32 devices in a mesh: section: 4 (over x, core), tp: 8 (over z, y).
Axes of the slice: x: 2, y: 2, z: 4, core: 2. Of those that a mesh axis runs over, the one named last changes fastest.
Arguments:
- patches: bfloat16 [2, 32, 4096], P(None, None, 'tp'), may hold values from -6 to 6
- table_ids: int32 [2, 32], replicated, may hold values from 0 to 32767
- lengths: int32 [2, 2], replicated, may hold values from 16 to 32
- embed_table: bfloat16 [32768, 4096], P('section', 'tp'), may hold values from -6 to 6
- norm_gain: bfloat16 [4, 4096], P('section'), may hold values from 0.099609375 to 1.8984375
- w_query: bfloat16 [4, 4096, 4096], P('section', None, 'tp'), may hold values from -0.09375 to 0.09375
- w_key: bfloat16 [4, 4096, 4096], P('section', None, 'tp'), may hold values from -0.09375 to 0.09375
- w_value: bfloat16 [4, 4096, 4096], P('section', None, 'tp'), may hold values from -0.09375 to 0.09375
- w_out: bfloat16 [4, 4096, 4096], P('section', None, 'tp'), may hold values from -0.09375 to 0.09375
Outputs:
- layer_rows: bfloat16 [4, 2, 32, 4096], P('section', None, None, 'tp')
The draws below stay inside these ranges and needn't reach their ends.
Inputs may be any that keep to these rules, and one draw needn't show every extreme that they name: `lengths`: column 0 counts a micro-batch's valid patches, column 1 its valid table tokens.
All inputs are finite; a program needn't handle non-finite values.
Results may differ from the reference program's by a relative error of at most 0.01.
Values may be sent and summed in bfloat16 or wider, within the bound.
No kernel may reach another device: no remote copies, remote signals or barrier semaphores. Data moves between devices by JAX's collectives and lax.ppermute only.
A program may use at most 64 MiB of HBM per device.

```python
import math
import jax
import jax.numpy as jnp
import numpy as np
from jax import lax

D = 4096
HEADS = 32
VOCAB = 32768
MICRO = 2
ROWS = 32
N_SECTION = 4


def place_ends(array, own_key, smallest, top_value):
    longest = array.shape.index(max(array.shape))
    spots = []
    for shift in (0, 1):
        where = [jax.random.randint(jax.random.fold_in(own_key, axis), (), 0, length) for axis, length in enumerate(array.shape)]
        where[longest] = (where[longest] + shift) % array.shape[longest]
        spots.append(tuple(where))
    return array.at[spots[0]].set(smallest).at[spots[1]].set(top_value)


def shard_levels(own_key, extent, split, least, high):
    def one(dim, parts):
        heights = jax.random.uniform(jax.random.fold_in(jax.random.fold_in(own_key, 6), dim), (parts,), jnp.float32, least / len(split), high / len(split))
        return jnp.repeat(jnp.exp(heights), extent[dim] // parts).reshape((-1,) + (1,) * (len(extent) - dim - 1))

    loudness = one(*split[0])
    for cut in split[1:]:
        loudness = loudness * one(*cut)
    return loudness


def rank_bounds(count, skew):
    portions = [(1 << 20) // math.isqrt(rank ** skew) + 1 for rank in range(1, count + 1)]
    width = 1 + sum(portions) // (1 << 30)
    return np.cumsum(np.array([max(1, weight // width) for weight in portions]))


def ranked(key, extent, number_of, lean):
    grid = rank_bounds(number_of, lean)
    ticket = jax.random.randint(jax.random.fold_in(key, 1), extent, 0, int(grid[number_of - 1]))
    grade = jnp.searchsorted(jnp.asarray(grid, jnp.int32), ticket, side="right")
    return jax.random.permutation(jax.random.fold_in(key, 2), number_of)[grade].astype(jnp.int32)


def gaussian(own_key, dims, deviation, bound, pieces=(), kind=jnp.bfloat16):
    factor_of = shard_levels(own_key, dims, pieces, -0.22, 0.18) if pieces else 1.0
    drawn = jax.random.normal(own_key, dims, jnp.float32) * deviation * factor_of
    return jnp.minimum(jnp.maximum(drawn, -bound), bound).astype(kind)


def setup_inputs(seed: int = 0) -> dict:
    arg_keys = jax.random.split(jax.random.key(seed), 10)
    patches = gaussian(arg_keys[0], (MICRO, ROWS, D), 1.0, 6.0, ((2, 8),))
    table_ids = place_ends(ranked(arg_keys[1], (MICRO, ROWS), VOCAB, 2), jax.random.fold_in(arg_keys[1], 3), 0, VOCAB - 1).astype(jnp.int32)
    lengths = place_ends(jax.random.randint(arg_keys[2], (MICRO, 2), ROWS // 2, ROWS + 1), jax.random.fold_in(arg_keys[2], 1), ROWS // 2, ROWS).astype(jnp.int32)
    embed_table = gaussian(arg_keys[3], (VOCAB, D), 1.0, 6.0, ((0, 4), (1, 8)))
    norm_gain = jnp.clip(1.0 + 0.18 * jax.random.normal(arg_keys[4], (N_SECTION, D), jnp.float32), 0.099609375, 1.8984375).astype(jnp.bfloat16)
    w_query = gaussian(arg_keys[5], (N_SECTION, D, D), D ** -0.5, 0.09375, ((0, 4), (2, 8)))
    w_key = gaussian(arg_keys[6], (N_SECTION, D, D), D ** -0.5, 0.09375, ((0, 4), (2, 8)))
    w_value = gaussian(arg_keys[7], (N_SECTION, D, D), D ** -0.5, 0.09375, ((0, 4), (2, 8)))
    w_out = gaussian(arg_keys[8], (N_SECTION, D, D), D ** -0.5, 0.09375, ((0, 4), (2, 8)))
    return dict(patches=patches, table_ids=table_ids, lengths=lengths, embed_table=embed_table, norm_gain=norm_gain, w_query=w_query, w_key=w_key, w_value=w_value, w_out=w_out)


epsilon = 1e-06

def run_layer(stream, gain_row, query_weight, key_weight, value_weight, out_weight, patch_count, table_count, encoder):
    head_dim = D // HEADS
    values_f = stream.astype(jnp.float32)
    inverse = lax.rsqrt(lax.optimization_barrier(jnp.mean(values_f * values_f, axis=-1, keepdims=True)) + epsilon)
    normed = (values_f * inverse * gain_row.astype(jnp.float32)).astype(jnp.bfloat16)
    if encoder:
        own_rows = normed[:ROWS]
        residual = stream[:ROWS]
    else:
        own_rows = normed[ROWS:]
        residual = stream[ROWS:]
    score_scale = 1.0 / math.sqrt(head_dim)
    query = (jnp.dot(own_rows, query_weight, preferred_element_type=jnp.float32) * score_scale).astype(jnp.bfloat16)
    key_rows = jnp.dot(normed, key_weight, preferred_element_type=jnp.float32).astype(jnp.bfloat16)
    value_rows = jnp.dot(normed, value_weight, preferred_element_type=jnp.float32).astype(jnp.bfloat16)
    query_heads = query.reshape(ROWS, HEADS, head_dim).astype(jnp.float32)
    key_heads = key_rows.reshape(2 * ROWS, HEADS, head_dim).astype(jnp.float32)
    value_heads = value_rows.reshape(2 * ROWS, HEADS, head_dim).astype(jnp.float32)
    scores = jnp.einsum('qhd,khd->hqk', query_heads, key_heads)
    query_pos = jnp.arange(ROWS, dtype=jnp.int32)[:, None]
    key_pos = jnp.arange(2 * ROWS, dtype=jnp.int32)[None, :]
    patch_mask = (key_pos < ROWS) & (key_pos < patch_count)
    if encoder:
        key_mask = patch_mask
    else:
        key_mask = patch_mask | (key_pos >= ROWS) & (key_pos - ROWS <= query_pos) & (key_pos - ROWS < table_count)
    exp_scores = jnp.where(key_mask[None], jnp.exp(scores), 0.0)
    weights = (exp_scores / lax.optimization_barrier(jnp.sum(exp_scores, axis=-1, keepdims=True))).astype(jnp.bfloat16)
    head_mix = jnp.einsum('hqk,khd->qhd', weights.astype(jnp.float32), value_heads)
    head_mix = head_mix.astype(jnp.bfloat16).reshape(ROWS, D)
    change = jnp.dot(head_mix, out_weight, preferred_element_type=jnp.float32)
    updated = (residual.astype(jnp.float32) + change).astype(jnp.bfloat16)
    if encoder:
        following = jnp.concatenate([updated, stream[ROWS:]], axis=0)
    else:
        following = jnp.concatenate([stream[:ROWS], updated], axis=0)
    return (updated, following)

def reference(patches, table_ids, lengths, embed_table, norm_gain, w_query, w_key, w_value, w_out):
    embedded = embed_table[table_ids]
    per_batch = []
    for batch_index in range(MICRO):
        stream = jnp.concatenate([patches[batch_index], embedded[batch_index]], axis=0)
        per_layer = []
        for layer_index in range(N_SECTION):
            updated, stream = run_layer(stream, norm_gain[layer_index], w_query[layer_index], w_key[layer_index], w_value[layer_index], w_out[layer_index], lengths[batch_index, 0], lengths[batch_index, 1], layer_index < N_SECTION // 2)
            per_layer.append(updated)
        per_batch.append(jnp.stack(per_layer))
    return jnp.stack(per_batch, axis=1)
```

```python
import math

import jax
import jax.numpy as jnp
from jax import lax
from jax.sharding import PartitionSpec as P

HEADS = 32


epsilon = 1e-06


def xor_groups(count):
    bits = [1 << i for i in reversed(range(count.bit_length() - 1))]
    first = len(bits) % 2
    groups = [bits[:first]] if first else []
    return groups + [bits[i : i + 2] for i in range(first, len(bits), 2)]


def gather_rows(block, axis):
    count = lax.axis_size(axis)
    me = lax.axis_index(axis)
    if count & (count - 1):
        return lax.all_gather(block, axis, axis=0, tiled=False)
    held = block[None]
    for bits in xor_groups(count):
        masks = [0]
        for bit in bits:
            masks = masks + [mask | bit for mask in masks]
        pieces = {0: held}
        for mask in sorted(masks[1:], reverse=True):
            route = [(i, i ^ mask) for i in range(count)]
            pieces[mask] = lax.ppermute(held, axis, route)
        for bit in bits:
            swap = (me & bit) != 0
            pieces = {
                mask: jnp.where(swap, pieces[mask ^ bit], pieces[mask]) for mask in pieces
            }
        held = jnp.stack([pieces[mask] for mask in sorted(masks)], axis=0)
    groups = xor_groups(count)
    shape = []
    for bits in reversed(groups):
        shape.append(1 << len(bits))
    held = held.reshape(tuple(shape) + block.shape)
    order = tuple(reversed(range(len(shape)))) + (len(shape), len(shape) + 1)
    return held.transpose(order).reshape((count,) + block.shape)


def side_by_side(stacked):
    count, rows, width = stacked.shape
    return stacked.transpose(1, 0, 2).reshape(rows, count * width)


def exchange(block, axis, first, second):
    index = lax.axis_index(axis)
    route = [(first, second), (second, first)]
    return lax.cond(
        (index == first) | (index == second),
        lambda rows: lax.ppermute(rows, axis, route),
        lambda rows: rows,
        block,
    )


def local(patches, table_ids, lengths, embed_table, norm_gain, w_query, w_key, w_value, w_out):
    section_count = lax.axis_size("section")
    section_index = lax.axis_index("section")
    half = section_count // 2
    micro_count, row_count, width_local = patches.shape
    width_full = w_query.shape[1]
    head_dim = width_full // HEADS
    heads_local = width_local // head_dim
    score_scale = 1.0 / math.sqrt(head_dim)
    query_weight = w_query[0]
    key_weight = w_key[0]
    value_weight = w_value[0]
    out_weight = w_out[0]
    gain_row = norm_gain[0].astype(jnp.float32)
    total_rows = micro_count * row_count
    vocab_local = embed_table.shape[0]

    def only(indices, body, operands, shape):
        taken = section_index == indices[0]
        for index in indices[1:]:
            taken = taken | (section_index == index)
        return lax.cond(taken, body, lambda *_: tuple(jnp.zeros(s, d) for s, d in shape), *operands)

    def look_up():
        local_ids = table_ids.reshape(-1) - section_index * vocab_local
        vocab_cols = lax.broadcasted_iota(jnp.int32, (total_rows, vocab_local), 1)
        one_hot = (local_ids[:, None] == vocab_cols).astype(jnp.bfloat16)
        return jnp.dot(one_hot, embed_table, preferred_element_type=jnp.float32).astype(
            jnp.bfloat16
        )

    def normalise(full):
        values_f = full.astype(jnp.float32)
        inverse = lax.rsqrt(jnp.mean(values_f * values_f, axis=-1, keepdims=True) + epsilon)
        return (values_f * inverse * gain_row).astype(jnp.bfloat16)

    def project(normed, weight):
        return jnp.dot(normed, weight, preferred_element_type=jnp.float32)

    def heads_of(rows):
        return rows.reshape(micro_count, row_count, heads_local, head_dim)

    def attend(query, keys, values, mask):
        scores = jnp.einsum("mqhd,mkhd->mhqk", query, keys, preferred_element_type=jnp.float32)
        exp_scores = jnp.where(mask[:, None], jnp.exp(scores), 0.0)
        weights = (exp_scores / jnp.sum(exp_scores, axis=-1, keepdims=True)).astype(jnp.bfloat16)
        mix = jnp.einsum("mhqk,mkhd->mqhd", weights, values, preferred_element_type=jnp.float32)
        return mix.astype(jnp.bfloat16).reshape(total_rows, width_local)

    def gathered(block):
        return side_by_side(gather_rows(block, "tp"))

    def finish(stream, mix):
        change = project(gathered(mix), out_weight)
        return (stream.astype(jnp.float32) + change).astype(jnp.bfloat16)

    def patch_mask(shape):
        key_pos = lax.broadcasted_iota(jnp.int32, shape, 2)
        return key_pos < lengths[:, 0][:, None, None]

    def encode(stream):
        normed = normalise(gathered(stream))
        query = heads_of((project(normed, query_weight) * score_scale).astype(jnp.bfloat16))
        keys = heads_of(project(normed, key_weight).astype(jnp.bfloat16))
        values = heads_of(project(normed, value_weight).astype(jnp.bfloat16))
        mask = patch_mask((micro_count, row_count, row_count))
        return (finish(stream, attend(query, keys, values, mask)),)

    def memory_rows(memory_full):
        normed = normalise(memory_full)
        keys = project(normed, key_weight).astype(jnp.bfloat16)
        values = project(normed, value_weight).astype(jnp.bfloat16)
        return keys, values

    def table_rows(stream):
        normed = normalise(gathered(stream))
        query = (project(normed, query_weight) * score_scale).astype(jnp.bfloat16)
        keys = project(normed, key_weight).astype(jnp.bfloat16)
        values = project(normed, value_weight).astype(jnp.bfloat16)
        return query, keys, values

    def decode(stream, memory_keys, memory_values, query, keys, values):
        shape = (micro_count, row_count, row_count)
        query_pos = lax.broadcasted_iota(jnp.int32, shape, 1)
        key_pos = lax.broadcasted_iota(jnp.int32, shape, 2)
        own = (key_pos <= query_pos) & (key_pos < lengths[:, 1][:, None, None])
        mask = jnp.concatenate([patch_mask(shape), own], axis=2)
        all_keys = jnp.concatenate([heads_of(memory_keys), heads_of(keys)], axis=1)
        all_values = jnp.concatenate([heads_of(memory_values), heads_of(values)], axis=1)
        mix = attend(heads_of(query), all_keys, all_values, mask)
        return (finish(stream, mix),)

    bf16 = jnp.bfloat16
    part = ((total_rows, width_local), bf16)
    whole = ((total_rows, width_full), bf16)

    def after(value, *earlier):
        return lax.optimization_barrier((value,) + earlier)[0]

    stream = patches.reshape(total_rows, width_local)
    (updated,) = only([0], encode, (stream,), (part,))
    result = updated
    rows_found = lax.cond(section_index != 0, look_up, lambda: jnp.zeros(*part))
    for index in range(1, section_count):
        if index != half:
            sent = exchange(rows_found, "section", index, half)
            rows_found = jnp.where(section_index == half, rows_found + sent, rows_found)
    stream = exchange(updated, "section", 0, 1)
    rows_found, stream = lax.optimization_barrier((rows_found, stream))
    own_found = lax.cond(section_index == 0, look_up, lambda: rows_found)
    sent = exchange(own_found, "section", 0, half)
    embedded = own_found + sent
    table = only([half], table_rows, (embedded,), (part, part, part))
    for index in range(1, half):
        (updated,) = only([index], encode, (stream,), (part,))
        result = jnp.where(section_index == index, updated, result)
        stream = exchange(updated, "section", index, index + 1)

    (memory,) = only([half], lambda block: (gathered(block),), (stream,), (whole,))
    stream = embedded
    for index in range(half, section_count):
        if index > half:
            memory_next = exchange(memory, "section", index - 1, index)
            memory = jnp.where(section_index == index, memory_next, memory)
        pair = only([index], memory_rows, (memory,), (part, part))
        if index > half:
            stream = exchange(after(stream, *pair), "section", index - 1, index)
            table = only([index], table_rows, (stream,), (part, part, part))
        (updated,) = only([index], decode, (stream, *pair, *table), (part,))
        result = jnp.where(section_index == index, updated, result)
        stream = updated
    return result.reshape(1, micro_count, row_count, width_local)


def solution(mesh):
    return jax.shard_map(
        local,
        mesh=mesh,
        in_specs=(
            P(None, None, "tp"),
            P(),
            P(),
            P("section", "tp"),
            P("section", None),
            P("section", None, "tp"),
            P("section", None, "tp"),
            P("section", None, "tp"),
            P("section", None, "tp"),
        ),
        out_specs=P("section", None, None, "tp"),
        check_vma=False,
    )
```

```python
import math

import jax
import jax.numpy as jnp
from jax import lax
from jax.sharding import PartitionSpec as P

HEADS = 32


epsilon = 1e-06


def xor_groups(count):
    bits = [1 << i for i in reversed(range(count.bit_length() - 1))]
    first = len(bits) % 2
    groups = [bits[:first]] if first else []
    return groups + [bits[i : i + 2] for i in range(first, len(bits), 2)]


def gather_rows(block, axis):
    count = lax.axis_size(axis)
    me = lax.axis_index(axis)
    if count & (count - 1):
        return lax.all_gather(block, axis, axis=0, tiled=False)
    held = block[None]
    for bits in xor_groups(count):
        masks = [0]
        for bit in bits:
            masks = masks + [mask | bit for mask in masks]
        pieces = {0: held}
        for mask in sorted(masks[1:], reverse=True):
            route = [(i, i ^ mask) for i in range(count)]
            pieces[mask] = lax.ppermute(held, axis, route)
        for bit in bits:
            swap = (me & bit) != 0
            pieces = {
                mask: jnp.where(swap, pieces[mask ^ bit], pieces[mask]) for mask in pieces
            }
        held = jnp.stack([pieces[mask] for mask in sorted(masks)], axis=0)
    groups = xor_groups(count)
    shape = []
    for bits in reversed(groups):
        shape.append(1 << len(bits))
    held = held.reshape(tuple(shape) + block.shape)
    order = tuple(reversed(range(len(shape)))) + (len(shape), len(shape) + 1)
    return held.transpose(order).reshape((count,) + block.shape)


def side_by_side(stacked):
    count, rows, width = stacked.shape
    return stacked.transpose(1, 0, 2).reshape(rows, count * width)


def exchange(block, axis, first, second):
    rest = [i for i in range(lax.axis_size(axis)) if i not in (first, second)]
    route = [(first, second), (second, first)]
    for i in range(0, len(rest) - 1, 2):
        route += [(rest[i], rest[i + 1]), (rest[i + 1], rest[i])]
    return lax.ppermute(block, axis, route)


def local(patches, table_ids, lengths, embed_table, norm_gain, w_query, w_key, w_value, w_out):
    section_count = lax.axis_size("section")
    section_index = lax.axis_index("section")
    half = section_count // 2
    micro_count, row_count, width_local = patches.shape
    width_full = w_query.shape[1]
    head_dim = width_full // HEADS
    heads_local = width_local // head_dim
    score_scale = 1.0 / math.sqrt(head_dim)
    query_weight = w_query[0]
    key_weight = w_key[0]
    value_weight = w_value[0]
    out_weight = w_out[0]
    total_rows = micro_count * row_count
    vocab_local = embed_table.shape[0]

    def only(indices, body, operands, shape):
        taken = section_index == indices[0]
        for index in indices[1:]:
            taken = taken | (section_index == index)
        return lax.cond(taken, body, lambda *_: tuple(jnp.zeros(s, d) for s, d in shape), *operands)

    def look_up():
        local_ids = table_ids.reshape(-1) - section_index * vocab_local
        vocab_cols = lax.broadcasted_iota(jnp.int32, (total_rows, vocab_local), 1)
        one_hot = (local_ids[:, None] == vocab_cols).astype(jnp.bfloat16)
        return jnp.dot(one_hot, embed_table, preferred_element_type=jnp.float32).astype(
            jnp.bfloat16
        )

    def normalise(full):
        values_f = full.astype(jnp.float32)
        inverse = lax.rsqrt(jnp.mean(values_f * values_f, axis=-1, keepdims=True) + epsilon)
        return (values_f * inverse * norm_gain[0].astype(jnp.float32)).astype(jnp.bfloat16)

    def project(normed, weight):
        return jnp.dot(normed, weight, preferred_element_type=jnp.float32)

    def heads_of(rows):
        return rows.reshape(micro_count, row_count, heads_local, head_dim)

    def attend(query, keys, values, mask):
        scores = jnp.einsum("mqhd,mkhd->mhqk", query, keys, preferred_element_type=jnp.float32)
        exp_scores = jnp.where(mask[:, None], jnp.exp(scores), 0.0)
        weights = (exp_scores / jnp.sum(exp_scores, axis=-1, keepdims=True)).astype(jnp.bfloat16)
        mix = jnp.einsum("mhqk,mkhd->mqhd", weights, values, preferred_element_type=jnp.float32)
        return mix.astype(jnp.bfloat16).reshape(total_rows, width_local)

    def gathered(block):
        return side_by_side(gather_rows(block, "tp"))

    def finish(stream, mix):
        change = project(gathered(mix), out_weight)
        return (stream.astype(jnp.float32) + change).astype(jnp.bfloat16)

    def patch_mask(shape):
        key_pos = lax.broadcasted_iota(jnp.int32, shape, 2)
        return key_pos < lengths[:, 0][:, None, None]

    def encode(stream):
        normed = normalise(gathered(stream))
        query = heads_of((project(normed, query_weight) * score_scale).astype(jnp.bfloat16))
        keys = heads_of(project(normed, key_weight).astype(jnp.bfloat16))
        values = heads_of(project(normed, value_weight).astype(jnp.bfloat16))
        mask = patch_mask((micro_count, row_count, row_count))
        return (finish(stream, attend(query, keys, values, mask)),)

    def memory_rows(memory_full):
        normed = normalise(memory_full)
        keys = project(normed, key_weight).astype(jnp.bfloat16)
        values = project(normed, value_weight).astype(jnp.bfloat16)
        return keys, values

    def table_rows(stream):
        normed = normalise(gathered(stream))
        query = (project(normed, query_weight) * score_scale).astype(jnp.bfloat16)
        keys = project(normed, key_weight).astype(jnp.bfloat16)
        values = project(normed, value_weight).astype(jnp.bfloat16)
        return query, keys, values

    def decode(stream, memory_keys, memory_values, query, keys, values):
        shape = (micro_count, row_count, row_count)
        query_pos = lax.broadcasted_iota(jnp.int32, shape, 1)
        key_pos = lax.broadcasted_iota(jnp.int32, shape, 2)
        own = (key_pos <= query_pos) & (key_pos < lengths[:, 1][:, None, None])
        mask = jnp.concatenate([patch_mask(shape), own], axis=2)
        all_keys = jnp.concatenate([heads_of(memory_keys), heads_of(keys)], axis=1)
        all_values = jnp.concatenate([heads_of(memory_values), heads_of(values)], axis=1)
        mix = attend(heads_of(query), all_keys, all_values, mask)
        return (finish(stream, mix),)

    bf16 = jnp.bfloat16
    part = ((total_rows, width_local), bf16)
    whole = ((total_rows, width_full), bf16)

    def after(value, *earlier):
        return lax.optimization_barrier((value,) + earlier)[0]

    def member(*indices):
        taken = section_index == indices[0]
        for index in indices[1:]:
            taken = taken | (section_index == index)
        return taken

    def look_up_and_add():
        found = look_up()
        others = list(range(1, section_count))
        total = found
        for shift in range(1, len(others)):
            route = [(s, others[(i + shift) % len(others)]) for i, s in enumerate(others)]
            total = total + lax.ppermute(found, "section", route)
        return total

    def embed(found):
        own = lax.cond(section_index == 0, look_up, lambda: found)
        sent = lax.ppermute(own, "section", [(0, half), (half, 0)])
        embedded = own + sent
        return (embedded, *only([half], table_rows, (embedded,), (part, part, part)))

    stream = patches.reshape(total_rows, width_local)
    (updated,) = only([0], encode, (stream,), (part,))
    result = updated
    found = lax.cond(section_index != 0, look_up_and_add, lambda: jnp.zeros(*part))
    table = None
    for index in range(half):
        if index:
            (updated,) = only([index], encode, (stream,), (part,))
            result = jnp.where(section_index == index, updated, result)
        earlier = (found,) if table is None else table
        stream = exchange(after(updated, *earlier), "section", index, index + 1)
        if table is None:
            table = only([0, half], embed, (after(found, stream),), (part,) * 4)
    embedded, *table = table

    (memory,) = only([half], lambda block: (gathered(block),), (stream,), (whole,))
    stream = embedded
    for index in range(half, section_count):
        pair = only([index], memory_rows, (memory,), (part, part))
        if index > half:
            stream = exchange(after(stream, *pair), "section", index - 1, index)
            table = only([index], table_rows, (stream,), (part, part, part))
        if index + 1 < section_count:
            memory = exchange(memory, "section", index, index + 1)
        (updated,) = only([index], decode, (stream, *pair, *table), (part,))
        result = jnp.where(section_index == index, updated, result)
        stream = updated
    return result.reshape(1, micro_count, row_count, width_local)


def solution(mesh):
    return jax.shard_map(
        local,
        mesh=mesh,
        in_specs=(
            P(None, None, "tp"),
            P(),
            P(),
            P("section", "tp"),
            P("section", None),
            P("section", None, "tp"),
            P("section", None, "tp"),
            P("section", None, "tp"),
            P("section", None, "tp"),
        ),
        out_specs=P("section", None, None, "tp"),
        check_vma=False,
    )
```

```python
import functools
import math

import jax
import jax.numpy as jnp
from jax import lax
from jax.experimental import pallas as pl
from jax.experimental.pallas import tpu as pltpu
from jax.sharding import PartitionSpec as P

HEADS = 32
PROJECT = ["query", "keys", "values"]


epsilon = 1e-06


def gather_steps(count):
    bits = [1 << i for i in reversed(range(count.bit_length() - 1))]
    steps = []
    while bits:
        if len(bits) % 2:
            steps.append([bits[0]])
            bits = bits[1:]
        else:
            steps.append([bits[1], bits[0], bits[0] | bits[1]])
            bits = bits[2:]
    return steps


def gather_pieces(block, axis):
    count = lax.axis_size(axis)
    held = [(block[None], [0])]
    for masks in gather_steps(count):
        if len(held) > 2:
            piece = jnp.concatenate([one for one, _ in held], axis=0)
            held = [(piece, [s for _, sources in held for s in sources])]
        received = []
        for piece, sources in held:
            for mask in masks:
                route = [(i, i ^ mask) for i in range(count)]
                received.append((lax.ppermute(piece, axis, route), [s ^ mask for s in sources]))
        held = held + received
    return held


def gather_masks(count):
    held = [[0]]
    for masks in gather_steps(count):
        if len(held) > 2:
            held = [[s for sources in held for s in sources]]
        held = held + [[s ^ mask for s in sources] for sources in held for mask in masks]
    return [s for sources in held for s in sources]


def exchange(block, axis, first, second):
    rest = [i for i in range(lax.axis_size(axis)) if i not in (first, second)]
    route = [(first, second), (second, first)]
    for i in range(0, len(rest) - 1, 2):
        route += [(rest[i], rest[i + 1]), (rest[i + 1], rest[i])]
    return lax.ppermute(block, axis, route)


def in_order(me_ref, pieces, sources, full_ref):
    for ref, masks in zip(pieces, sources):
        width = ref.shape[2]
        for i, mask in enumerate(masks):
            start = pl.multiple_of((me_ref[0] ^ mask) * width, width)
            full_ref[:, pl.ds(start, width)] = ref[i]


def normalise_into(full_ref, gain_ref, normed_ref):
    width = full_ref.shape[1]
    tile = min(width, 512)
    total = jnp.zeros((full_ref.shape[0], 128), jnp.float32)
    for start in range(0, width, 128):
        part = full_ref[:, start : start + 128].astype(jnp.float32)
        total = total + part * part
    mean = jnp.sum(total, axis=1, keepdims=True) * (1.0 / width)
    inverse = lax.rsqrt(mean + epsilon)
    for start in range(0, width, tile):
        columns = slice(start, start + tile)
        gain = gain_ref[:, columns].astype(jnp.float32)
        normed_ref[:, columns] = (
            full_ref[:, columns].astype(jnp.float32) * inverse * gain
        ).astype(jnp.bfloat16)


def multiply_into(rows_ref, weight_ref, store):
    width = weight_ref.shape[1]
    tile = min(width, 256)

    @pl.loop(0, width // tile)
    def _(step):
        columns = pl.ds(pl.multiple_of(step * tile, tile), tile)
        store(
            columns,
            jnp.dot(rows_ref[...], weight_ref[:, columns], preferred_element_type=jnp.float32),
        )


def attend_into(lengths_ref, row_count, head_dim, query_ref, blocks, mix_ref):
    shape = (row_count, row_count)
    query_pos = lax.broadcasted_iota(jnp.int32, shape, 0)
    key_pos = lax.broadcasted_iota(jnp.int32, shape, 1)
    for micro in range(query_ref.shape[0] // row_count):
        rows = slice(micro * row_count, (micro + 1) * row_count)
        allowed = []
        for _, _, is_table in blocks:
            if is_table:
                allowed.append((key_pos <= query_pos) & (key_pos < lengths_ref[micro, 1]))
            else:
                allowed.append(key_pos < lengths_ref[micro, 0])
        for start in range(0, query_ref.shape[1], head_dim):
            columns = slice(start, start + head_dim)
            query = query_ref[rows, columns]
            exps = []
            for (keys_ref, _, _), mask in zip(blocks, allowed):
                scores = lax.dot_general(
                    query,
                    keys_ref[rows, columns],
                    (((1,), (1,)), ((), ())),
                    preferred_element_type=jnp.float32,
                )
                exps.append(jnp.where(mask, jnp.exp(scores), 0.0))
            total = sum(jnp.sum(one, axis=1, keepdims=True) for one in exps)
            mix = None
            for one, (_, values_ref, _) in zip(exps, blocks):
                weights = (one / total).astype(jnp.bfloat16)
                part = jnp.dot(
                    weights, values_ref[rows, columns], preferred_element_type=jnp.float32
                )
                mix = part if mix is None else mix + part
            mix_ref[rows, columns] = mix.astype(jnp.bfloat16)


def layer_kernel(plan, *refs):
    refs = list(refs)
    me_ref, lengths_ref = refs[:2]
    pieces = refs[2 : 2 + len(plan["sources"])]
    refs = refs[2 + len(plan["sources"]) :]
    gain_ref, refs = refs[0], refs[1:]
    weights, refs = refs[: len(plan["project"])], refs[len(plan["project"]) :]
    given, refs = refs[: len(plan["given"])], refs[len(plan["given"]) :]
    out_ref, full_ref, normed_ref = refs[:3]
    held = {}
    for ref, names in zip(given, plan["given"]):
        for i, name in enumerate(names):
            held[name] = ref.at[i]
    targets = refs[3:] if plan["attend"] else [out_ref.at[i] for i in range(len(weights))]
    if not plan["attend"] and plan["keep_own"]:
        out_ref[len(weights)] = pieces[0][0]
    in_order(me_ref, pieces, plan["sources"], full_ref)
    normalise_into(full_ref, gain_ref, normed_ref)
    for name, weight_ref, target in zip(plan["project"], weights, targets):
        scale = plan["scale"] if name == "query" else None

        def store(columns, value, target=target, scale=scale):
            if scale is not None:
                value = value * scale
            target[:, columns] = value.astype(jnp.bfloat16)

        multiply_into(normed_ref, weight_ref, store)
        held[name] = target
    if plan["attend"]:
        blocks = [(held["keys" + tag], held["values" + tag], is_table)
                  for tag, is_table in plan["attend"]]
        attend_into(
            lengths_ref, plan["rows"], plan["head_dim"], held["query"], blocks, out_ref
        )


def project_kernel(sources, me_ref, *refs):
    pieces, refs = refs[: len(sources)], refs[len(sources) :]
    weight_ref, stream_ref, out_ref, full_ref = refs
    in_order(me_ref, pieces, sources, full_ref)

    def store(columns, value):
        out_ref[:, columns] = (stream_ref[:, columns].astype(jnp.float32) + value).astype(
            jnp.bfloat16
        )

    multiply_into(full_ref, weight_ref, store)


VMEM = pl.BlockSpec(memory_space=pltpu.VMEM)
SMEM = pl.BlockSpec(memory_space=pltpu.SMEM)


def load_kernel(weight_ref, _, out_ref, sem):
    copy = pltpu.make_async_copy(weight_ref, out_ref, sem)
    copy.start()
    copy.wait()


def load(weight, earlier):
    size = 2 * weight.size
    return pl.pallas_call(
        load_kernel,
        out_shape=pltpu.VMEM(weight.shape, weight.dtype),
        in_specs=[pl.BlockSpec(memory_space=pl.ANY)] * 2,
        out_specs=VMEM,
        scratch_shapes=[pltpu.SemaphoreType.DMA(())],
        compiler_params=pltpu.CompilerParams(vmem_limit_bytes=1 << 20),
        cost_estimate=pl.CostEstimate(flops=0, bytes_accessed=2 * size, transcendentals=0),
    )(weight, earlier)


def near(array):
    return pltpu.with_memory_space_constraint(array, pltpu.VMEM)


def local(patches, table_ids, lengths, embed_table, norm_gain, w_query, w_key, w_value, w_out):
    section_count = lax.axis_size("section")
    section_index = lax.axis_index("section")
    half = section_count // 2
    micro_count, row_count, width_local = patches.shape
    width_full = w_query.shape[1]
    head_dim = width_full // HEADS
    score_scale = 1.0 / math.sqrt(head_dim)
    weight_of = {"query": w_query[0], "keys": w_key[0], "values": w_value[0]}
    out_weight = w_out[0]
    total_rows = micro_count * row_count
    vocab_local = embed_table.shape[0]
    me = lax.axis_index("tp").reshape(1)
    bf16 = jnp.bfloat16
    part = ((total_rows, width_local), bf16)

    def only(indices, body, operands, shape):
        return lax.cond(
            member(*indices), body, lambda *_: tuple(jnp.zeros(s, d) for s, d in shape), *operands
        )

    def member(*indices):
        taken = section_index == indices[0]
        for index in indices[1:]:
            taken = taken | (section_index == index)
        return taken

    def after(value, *earlier):
        return lax.optimization_barrier((value,) + earlier)[0]

    def look_up():
        local_ids = table_ids.reshape(-1) - section_index * vocab_local
        vocab_cols = lax.broadcasted_iota(jnp.int32, (total_rows, vocab_local), 1)
        one_hot = (local_ids[:, None] == vocab_cols).astype(bf16)
        return jnp.dot(one_hot, embed_table, preferred_element_type=jnp.float32).astype(bf16)

    def gather_and_load(block, project):
        held = gather_pieces(block, "tp")
        moments = [held[0][0], held[1][0], held[1][0]]
        return held, [load(weight_of[n], m) for n, m in zip(project, moments)]

    def layer(held, project, weights=None, given=(), attend=None, keep_own=False):
        plan = {
            "sources": [masks for _, masks in held],
            "project": project,
            "given": [names for _, names in given],
            "attend": attend,
            "keep_own": keep_own,
            "scale": score_scale,
            "rows": row_count,
            "head_dim": head_dim,
        }
        scratch = [pltpu.VMEM((total_rows, width_full), bf16)] * 2
        out_shape = part[0] if attend else (len(project) + keep_own,) + part[0]
        if attend:
            scratch += [pltpu.VMEM(*part)] * len(project)
        return pl.pallas_call(
            functools.partial(layer_kernel, plan),
            out_shape=jax.ShapeDtypeStruct(out_shape, bf16),
            in_specs=[SMEM, SMEM] + [VMEM] * (len(held) + 1 + len(project) + len(given)),
            out_specs=VMEM,
            scratch_shapes=scratch,
            compiler_params=pltpu.CompilerParams(vmem_limit_bytes=8 << 20),
            cost_estimate=pl.CostEstimate(
                flops=2 * total_rows * width_full * width_local * len(project),
                bytes_accessed=2 * width_full * width_local * len(project),
                transcendentals=0,
            ),
        )(
            me,
            lengths,
            *[piece for piece, _ in held],
            norm_gain,
            *(weights or [near(weight_of[name]) for name in project]),
            *[rows for rows, _ in given],
        )

    def finish(stream, mix):
        held = gather_pieces(mix, "tp")
        return pl.pallas_call(
            functools.partial(project_kernel, [masks for _, masks in held]),
            out_shape=jax.ShapeDtypeStruct(*part),
            in_specs=[SMEM] + [VMEM] * (len(held) + 2),
            out_specs=VMEM,
            scratch_shapes=[pltpu.VMEM((total_rows, width_full), bf16)],
            compiler_params=pltpu.CompilerParams(vmem_limit_bytes=8 << 20),
            cost_estimate=pl.CostEstimate(
                flops=2 * total_rows * width_full * width_local,
                bytes_accessed=2 * width_full * width_local,
                transcendentals=0,
            ),
        )(me, *[piece for piece, _ in held], near(out_weight), stream)

    def encode(stream):
        held, weights = gather_and_load(stream, PROJECT)
        mix = layer(held, PROJECT, weights, attend=[("", False)])
        return (finish(stream, mix),)

    def embed(found):
        own = lax.cond(section_index == 0, look_up, lambda: found)
        sent = lax.ppermute(own, "section", [(0, half), (half, 0)])
        return only(
            [half],
            lambda rows: (layer(gather_pieces(rows, "tp"), PROJECT, keep_own=True),),
            (own + sent,),
            (table_part,),
        )

    def look_up_and_add():
        found = look_up()
        others = list(range(1, section_count))
        total = found
        for shift in range(1, len(others)):
            route = [(s, others[(i + shift) % len(others)]) for i, s in enumerate(others)]
            total = total + lax.ppermute(found, "section", route)
        return total

    def stack(held):
        return jnp.concatenate([piece for piece, _ in held], axis=0)

    table_part = ((len(PROJECT) + 1,) + part[0], bf16)
    memory_part = ((lax.axis_size("tp"),) + part[0], bf16)
    memory_masks = gather_masks(lax.axis_size("tp"))
    pair_part = ((2,) + part[0], bf16)

    stream = patches.reshape(total_rows, width_local)
    (updated,) = only([0], encode, (stream,), (part,))
    result = updated
    found = lax.cond(section_index != 0, look_up_and_add, lambda: jnp.zeros(*part))
    table = None
    for index in range(half):
        if index:
            (updated,) = only([index], encode, (stream,), (part,))
            result = jnp.where(section_index == index, updated, result)
        stream = exchange(
            after(updated, found if table is None else table), "section", index, index + 1
        )
        if table is None:
            (table,) = only([0, half], embed, (after(found, stream),), (table_part,))

    (memory,) = only(
        [half], lambda rows: (stack(gather_pieces(rows, "tp")),), (stream,), (memory_part,)
    )
    for index in range(half, section_count):
        received = memory
        if index > half:
            (pair,) = only(
                [index],
                lambda rows: (layer([(rows, memory_masks)], ["keys", "values"]),),
                (received,),
                (pair_part,),
            )
            stream = exchange(after(updated, pair), "section", index - 1, index)
        if index + 1 < section_count:
            memory = exchange(memory, "section", index, index + 1)
        if index == half:

            def decode(rows, table):
                mix = layer(
                    [(rows, memory_masks)],
                    ["keys", "values"],
                    given=[(table, ["query", "keys_t", "values_t", "own"])],
                    attend=[("", False), ("_t", True)],
                )
                return (finish(table[len(PROJECT)], mix),)

            (updated,) = only([index], decode, (received, table), (part,))
        else:

            def decode(stream, pair):
                held, weights = gather_and_load(stream, PROJECT)
                mix = layer(
                    held,
                    PROJECT,
                    weights,
                    given=[(pair, ["keys_m", "values_m"])],
                    attend=[("_m", False), ("", True)],
                )
                return (finish(stream, mix),)

            (updated,) = only([index], decode, (stream, pair), (part,))
        result = jnp.where(section_index == index, updated, result)
    return result.reshape(1, micro_count, row_count, width_local)


def solution(mesh):
    return jax.shard_map(
        local,
        mesh=mesh,
        in_specs=(
            P(None, None, "tp"),
            P(),
            P(),
            P("section", "tp"),
            P("section", None),
            P("section", None, "tp"),
            P("section", None, "tp"),
            P("section", None, "tp"),
            P("section", None, "tp"),
        ),
        out_specs=P("section", None, None, "tp"),
        check_vma=False,
    )
```

```python
import math

import jax
import jax.numpy as jnp
from jax import lax
from jax.experimental import pallas as pl
from jax.sharding import PartitionSpec as P

HEADS = 32


epsilon = 1e-06


def gather_steps(count):
    bits = [1 << i for i in reversed(range(count.bit_length() - 1))]
    steps = []
    while bits:
        if len(bits) % 2:
            steps.append([bits[0]])
            bits = bits[1:]
        else:
            steps.append([bits[0] | bits[1], bits[0], bits[1]])
            bits = bits[2:]
    return steps


def gather_rows(block, axis):
    count = lax.axis_size(axis)
    me = lax.axis_index(axis)
    held = [(block[None], [0])]
    for masks in gather_steps(count):
        if len(held) > 2:
            piece = jnp.concatenate([one for one, _ in held], axis=0)
            held = [(piece, [s for _, sources in held for s in sources])]
        received = []
        for piece, sources in held:
            for mask in masks:
                route = [(i, i ^ mask) for i in range(count)]
                received.append((lax.ppermute(piece, axis, route), [s ^ mask for s in sources]))
        held = held + received
    pieces = {
        mask: piece[i] for piece, sources in held for i, mask in enumerate(sources)
    }
    for bit in [1 << i for i in reversed(range(count.bit_length() - 1))]:
        swap = (me & bit) != 0
        pieces = {m: jnp.where(swap, pieces[m ^ bit], pieces[m]) for m in pieces}
    return jnp.concatenate([pieces[m] for m in sorted(pieces)], axis=1)


def exchange(block, axis, pairs):
    used = [index for pair in pairs for index in pair]
    rest = [index for index in range(lax.axis_size(axis)) if index not in used]
    pairs = list(pairs) + list(zip(rest[0::2], rest[1::2]))
    route = [way for first, second in pairs for way in ((first, second), (second, first))]
    return lax.ppermute(block, axis, route)


def nothing(*shapes):
    specs = [pl.BlockSpec(memory_space=pl.ANY)] * len(shapes)
    return pl.pallas_call(
        lambda *refs: None,
        out_shape=[jax.ShapeDtypeStruct(shape, jnp.bfloat16) for shape in shapes],
        out_specs=specs,
    )()


def local(patches, table_ids, lengths, embed_table, norm_gain, w_query, w_key, w_value, w_out):
    section_count = lax.axis_size("section")
    section_index = lax.axis_index("section")
    half = section_count // 2
    micro_count, row_count, width_local = patches.shape
    width_full = w_query.shape[1]
    head_dim = width_full // HEADS
    heads_local = width_local // head_dim
    score_scale = 1.0 / math.sqrt(head_dim)
    own_weights = (norm_gain[0], w_query[0], w_key[0], w_value[0])
    total_rows = micro_count * row_count
    vocab_local = embed_table.shape[0]
    bf16 = jnp.bfloat16
    part = (total_rows, width_local)
    whole = (total_rows, width_full)

    def member(*indices):
        taken = section_index == indices[0]
        for index in indices[1:]:
            taken = taken | (section_index == index)
        return taken

    def only(indices, body, operands, *shapes):
        return lax.cond(member(*indices), body, lambda *_: tuple(nothing(*shapes)), *operands)

    def after(value, *earlier):
        return lax.optimization_barrier((value,) + earlier)[0]

    def look_up():
        local_ids = table_ids.reshape(-1) - section_index * vocab_local
        vocab_cols = lax.broadcasted_iota(jnp.int32, (total_rows, vocab_local), 1)
        one_hot = (local_ids[:, None] == vocab_cols).astype(bf16)
        return jnp.dot(one_hot, embed_table, preferred_element_type=jnp.float32).astype(bf16)

    def look_up_and_add():
        found = look_up()
        others = list(range(1, section_count))
        total = found
        for shift in range(1, len(others)):
            route = [(s, others[(i + shift) % len(others)]) for i, s in enumerate(others)]
            total = total + lax.ppermute(found, "section", route)
        return (total,)

    def normalise(full, gain):
        values_f = full.astype(jnp.float32)
        inverse = lax.rsqrt(jnp.mean(values_f * values_f, axis=-1, keepdims=True) + epsilon)
        return (values_f * inverse * gain.astype(jnp.float32)).astype(bf16)

    def multiply(rows, weight):
        return jnp.dot(rows, weight, preferred_element_type=jnp.float32)

    def project(full, weights):
        gain, query_weight, key_weight, value_weight = weights
        normed = normalise(full, gain)
        return (
            (multiply(normed, query_weight) * score_scale).astype(bf16),
            multiply(normed, key_weight).astype(bf16),
            multiply(normed, value_weight).astype(bf16),
        )

    def heads_of(rows):
        return rows.reshape(micro_count, row_count, heads_local, head_dim)

    def attend(query, keys, values, mask):
        scores = jnp.einsum("mqhd,mkhd->mhqk", query, keys, preferred_element_type=jnp.float32)
        exp_scores = jnp.where(mask[:, None], jnp.exp(scores), 0.0)
        weights = (exp_scores / jnp.sum(exp_scores, axis=-1, keepdims=True)).astype(bf16)
        mix = jnp.einsum("mhqk,mkhd->mqhd", weights, values, preferred_element_type=jnp.float32)
        return mix.astype(bf16).reshape(part)

    mask_shape = (micro_count, row_count, row_count)

    def patch_mask():
        key_pos = lax.broadcasted_iota(jnp.int32, mask_shape, 2)
        return key_pos < lengths[:, 0][:, None, None]

    def encoder_mix(query, keys, values):
        return attend(heads_of(query), heads_of(keys), heads_of(values), patch_mask())

    def decoder_mix(memory_keys, memory_values, query, keys, values):
        query_pos = lax.broadcasted_iota(jnp.int32, mask_shape, 1)
        key_pos = lax.broadcasted_iota(jnp.int32, mask_shape, 2)
        own = (key_pos <= query_pos) & (key_pos < lengths[:, 1][:, None, None])
        return attend(
            heads_of(query),
            jnp.concatenate([heads_of(memory_keys), heads_of(keys)], axis=1),
            jnp.concatenate([heads_of(memory_values), heads_of(values)], axis=1),
            jnp.concatenate([patch_mask(), own], axis=2),
        )

    def finish(stream, mix, out_weight):
        change = multiply(gather_rows(mix, "tp"), out_weight)
        return ((stream.astype(jnp.float32) + change).astype(bf16),)

    def gather_and_project(stream, *weights):
        return project(gather_rows(stream, "tp"), weights)

    def encoder_finish(stream, query, keys, values, out_weight):
        return finish(stream, encoder_mix(query, keys, values), out_weight)

    def decoder_finish(stream, memory_keys, memory_values, query, keys, values, out_weight):
        mix = decoder_mix(memory_keys, memory_values, query, keys, values)
        return finish(stream, mix, out_weight)

    def memory_project(stream, gain, key_weight, value_weight):
        memory = gather_rows(stream, "tp")
        normed = normalise(memory, gain)
        keys, values = multiply(normed, key_weight), multiply(normed, value_weight)
        return memory, keys.astype(bf16), values.astype(bf16)

    def both_project(memory, stream, *weights):
        gain, query_weight, key_weight, value_weight = weights
        normed = normalise(gather_rows(stream, "tp"), gain)
        rows = jnp.concatenate([normalise(memory, gain), normed], axis=0)
        keys, values = multiply(rows, key_weight), multiply(rows, value_weight)
        query = (multiply(normed, query_weight) * score_scale).astype(bf16)
        keys, values = keys.astype(bf16), values.astype(bf16)
        return (
            keys[:total_rows],
            values[:total_rows],
            query,
            keys[total_rows:],
            values[total_rows:],
        )

    pairs = [(index, index + 1) for index in range(0, section_count, 2)]

    def swap_weights(*weights):
        route = [way for first, second in pairs[1:] for way in ((first, second), (second, first))]
        return tuple(lax.ppermute(weight, "section", route) for weight in weights)

    def embed(found):
        own = lax.cond(section_index == 0, look_up, lambda: found)
        embedded = own + lax.ppermute(own, "section", [(0, half), (half, 0)])
        (table,) = only(
            [half],
            lambda rows, *weights: (jnp.stack(gather_and_project(rows, *weights) + (rows,)),),
            (embedded, *own_weights),
            (4,) + part,
        )
        return (table,)

    out_swapped = exchange(w_out[0], "section", pairs)
    first = patches.reshape(part)
    (mix,) = only(
        [0],
        lambda rows, *weights: (encoder_mix(*gather_and_project(rows, *weights)),),
        (first, *own_weights),
        part,
    )
    (found,) = lax.cond(
        section_index != 0, look_up_and_add, lambda: tuple(nothing(part))
    )
    swapped = lax.cond(
        section_index >= 2,
        swap_weights,
        lambda *_: tuple(nothing(*[weight.shape for weight in own_weights])),
        after(norm_gain[0], found),
        *own_weights[1:],
    )
    mix = exchange(after(mix, found, *swapped), "section", pairs)
    (table,) = only([0, half], embed, (after(found, mix),), (4,) + part)
    table = lax.cond(
        member(half, half + 1),
        lambda rows: lax.ppermute(rows, "section", [(half, half + 1), (half + 1, half)]),
        lambda rows: nothing(rows.shape)[0],
        table,
    )

    result = None
    for even in range(0, section_count, 2):
        odd = even + 1
        if even == 0:
            (updated,) = only([odd], finish, (first, mix, out_swapped), part)
        elif even < half:
            heads = only([odd], gather_and_project, (stream, *swapped), part, part, part)
            (updated,) = only([odd], encoder_finish, (stream, *heads, out_swapped), part)
        elif even == half:
            gain, _, key_weight, value_weight = swapped
            memory, *pair = only(
                [odd], memory_project, (stream, gain, key_weight, value_weight), whole, part, part
            )
            (updated,) = only(
                [odd],
                lambda rows, *rest: decoder_finish(
                    rows[3], rest[0], rest[1], rows[0], rows[1], rows[2], rest[2]
                ),
                (table, *pair, out_swapped),
                part,
            )
        else:
            heads = only([odd], both_project, (memory, stream, *swapped), *[part] * 5)
            (updated,) = only([odd], decoder_finish, (stream, *heads, out_swapped), part)
        returned = exchange(updated, "section", pairs)
        stream = updated
        if even < half:
            heads = only([odd], gather_and_project, (stream, *own_weights), part, part, part)
            (updated,) = only([odd], encoder_finish, (stream, *heads, w_out[0]), part)
        else:
            heads = only([odd], both_project, (memory, stream, *own_weights), *[part] * 5)
            (updated,) = only([odd], decoder_finish, (stream, *heads, w_out[0]), part)
        mine = jnp.where(section_index == odd, updated, returned)
        result = mine if result is None else jnp.where(section_index >= even, mine, result)
        if odd + 1 < section_count:
            ahead = [(odd, odd + 2), (even, even + 2)]
            if even >= half:
                memory = exchange(memory, "section", ahead)
            else:
                updated = after(updated, table)
            stream = exchange(updated, "section", ahead)
    return result.reshape(1, micro_count, row_count, width_local)


def solution(mesh):
    return jax.shard_map(
        local,
        mesh=mesh,
        in_specs=(
            P(None, None, "tp"),
            P(),
            P(),
            P("section", "tp"),
            P("section", None),
            P("section", None, "tp"),
            P("section", None, "tp"),
            P("section", None, "tp"),
            P("section", None, "tp"),
        ),
        out_specs=P("section", None, None, "tp"),
        check_vma=False,
    )
```

```python
import math

import jax
import jax.numpy as jnp
from jax import lax
from jax.experimental import pallas as pl
from jax.sharding import PartitionSpec as P

HEADS = 32


epsilon = 1e-06


def gather_steps(count):
    bits = [1 << i for i in reversed(range(count.bit_length() - 1))]
    steps = []
    while bits:
        if len(bits) % 2:
            steps.append([bits[0]])
            bits = bits[1:]
        else:
            steps.append([bits[0] | bits[1], bits[0], bits[1]])
            bits = bits[2:]
    return steps


def gather_rows(block, axis):
    count = lax.axis_size(axis)
    me = lax.axis_index(axis)
    held = [(block[None], [0])]
    for masks in gather_steps(count):
        if len(held) > 2:
            piece = jnp.concatenate([one for one, _ in held], axis=0)
            held = [(piece, [s for _, sources in held for s in sources])]
        received = []
        for piece, sources in held:
            for mask in masks:
                route = [(i, i ^ mask) for i in range(count)]
                received.append((lax.ppermute(piece, axis, route), [s ^ mask for s in sources]))
        held = held + received
    pieces = {
        mask: piece[i] for piece, sources in held for i, mask in enumerate(sources)
    }
    for bit in [1 << i for i in reversed(range(count.bit_length() - 1))]:
        swap = (me & bit) != 0
        pieces = {m: jnp.where(swap, pieces[m ^ bit], pieces[m]) for m in pieces}
    return jnp.concatenate([pieces[m] for m in sorted(pieces)], axis=1)


def exchange(block, axis, pairs):
    used = [index for pair in pairs for index in pair]
    rest = [index for index in range(lax.axis_size(axis)) if index not in used]
    pairs = list(pairs) + list(zip(rest[0::2], rest[1::2]))
    route = [way for first, second in pairs for way in ((first, second), (second, first))]
    return lax.ppermute(block, axis, route)


def nothing(*shapes):
    specs = [pl.BlockSpec(memory_space=pl.ANY)] * len(shapes)
    return pl.pallas_call(
        lambda *refs: None,
        out_shape=[jax.ShapeDtypeStruct(shape, jnp.bfloat16) for shape in shapes],
        out_specs=specs,
    )()


def long_start(rows):
    mark = pl.pallas_call(
        lambda *refs: None,
        out_shape=jax.ShapeDtypeStruct((8, 128), jnp.float32),
        in_specs=[pl.BlockSpec(memory_space=pl.ANY)],
        out_specs=pl.BlockSpec(memory_space=pl.ANY),
        cost_estimate=pl.CostEstimate(flops=40 * 10**9, bytes_accessed=0, transcendentals=0),
    )(rows)
    return lax.optimization_barrier((rows, mark))[0]


def local(patches, table_ids, lengths, embed_table, norm_gain, w_query, w_key, w_value, w_out):
    section_count = lax.axis_size("section")
    section_index = lax.axis_index("section")
    half = section_count // 2
    micro_count, row_count, width_local = patches.shape
    width_full = w_query.shape[1]
    head_dim = width_full // HEADS
    heads_local = width_local // head_dim
    score_scale = 1.0 / math.sqrt(head_dim)
    own_weights = (norm_gain, w_query[0], w_key[0], w_value[0], w_out[0])
    total_rows = micro_count * row_count
    vocab_local = embed_table.shape[0]
    bf16 = jnp.bfloat16
    part = (total_rows, width_local)
    whole = (total_rows, width_full)

    def member(*indices):
        taken = section_index == indices[0]
        for index in indices[1:]:
            taken = taken | (section_index == index)
        return taken

    def only(indices, body, operands, *shapes):
        return lax.cond(member(*indices), body, lambda *_: tuple(nothing(*shapes)), *operands)

    def after(value, *earlier):
        return lax.optimization_barrier((value,) + earlier)[0]

    def look_up():
        local_ids = table_ids.reshape(-1) - section_index * vocab_local
        vocab_cols = lax.broadcasted_iota(jnp.int32, (total_rows, vocab_local), 1)
        one_hot = (local_ids[:, None] == vocab_cols).astype(bf16)
        return jnp.dot(one_hot, embed_table, preferred_element_type=jnp.float32).astype(bf16)

    def look_up_and_add():
        found = look_up()
        others = list(range(1, section_count))
        total = found
        for shift in range(1, len(others)):
            route = [(s, others[(i + shift) % len(others)]) for i, s in enumerate(others)]
            total = total + lax.ppermute(found, "section", route)
        return (total,)

    def normalise(full, gain):
        values_f = full.astype(jnp.float32)
        inverse = lax.rsqrt(jnp.mean(values_f * values_f, axis=-1, keepdims=True) + epsilon)
        return (values_f * inverse * gain.astype(jnp.float32)).astype(bf16)

    def multiply(rows, weight):
        return jnp.dot(rows, weight, preferred_element_type=jnp.float32)

    def project(full, weights):
        gain, query_weight, key_weight, value_weight = weights
        normed = normalise(full, gain)
        return (
            (multiply(normed, query_weight) * score_scale).astype(bf16),
            multiply(normed, key_weight).astype(bf16),
            multiply(normed, value_weight).astype(bf16),
        )

    def heads_of(rows):
        return rows.reshape(micro_count, row_count, heads_local, head_dim)

    def attend(query, keys, values, mask):
        scores = jnp.einsum("mqhd,mkhd->mhqk", query, keys, preferred_element_type=jnp.float32)
        exp_scores = jnp.where(mask[:, None], jnp.exp(scores), 0.0)
        weights = (exp_scores / jnp.sum(exp_scores, axis=-1, keepdims=True)).astype(bf16)
        mix = jnp.einsum("mhqk,mkhd->mqhd", weights, values, preferred_element_type=jnp.float32)
        return mix.astype(bf16).reshape(part)

    mask_shape = (micro_count, row_count, row_count)

    def patch_mask():
        key_pos = lax.broadcasted_iota(jnp.int32, mask_shape, 2)
        return key_pos < lengths[:, 0][:, None, None]

    def encoder_mix(query, keys, values):
        return attend(heads_of(query), heads_of(keys), heads_of(values), patch_mask())

    def decoder_mix(memory_keys, memory_values, query, keys, values):
        query_pos = lax.broadcasted_iota(jnp.int32, mask_shape, 1)
        key_pos = lax.broadcasted_iota(jnp.int32, mask_shape, 2)
        own = (key_pos <= query_pos) & (key_pos < lengths[:, 1][:, None, None])
        return attend(
            heads_of(query),
            jnp.concatenate([heads_of(memory_keys), heads_of(keys)], axis=1),
            jnp.concatenate([heads_of(memory_values), heads_of(values)], axis=1),
            jnp.concatenate([patch_mask(), own], axis=2),
        )

    def finish(stream, mix, out_weight):
        change = multiply(gather_rows(mix, "tp"), out_weight)
        return (stream.astype(jnp.float32) + change).astype(bf16)

    def encode(stream, *weights):
        stream = long_start(stream)
        mix = encoder_mix(*project(gather_rows(stream, "tp"), weights[:4]))
        return (finish(stream, mix, weights[4]),)

    def memory_project(memory, weights):
        gain, _, key_weight, value_weight, _ = weights
        normed = normalise(memory, gain)
        keys, values = multiply(normed, key_weight), multiply(normed, value_weight)
        return keys.astype(bf16), values.astype(bf16)

    def table_project(stream, *weights):
        heads = project(gather_rows(stream, "tp"), weights[:4])
        return (jnp.stack(heads + (stream,)),)

    def first_decode(memory, table, weights, following):
        memory = gather_rows(long_start(memory), "tp")
        mix = decoder_mix(*memory_project(memory, weights), table[0], table[1], table[2])
        updated = finish(table[3], mix, weights[4])
        return (updated, *memory_project(memory, following), memory)

    def decode(stream, keys, values, *weights):
        stream = long_start(stream)
        heads = project(gather_rows(stream, "tp"), weights[:4])
        return (finish(stream, decoder_mix(keys, values, *heads), weights[4]),)

    pairs = [(index, index + 1) for index in range(0, section_count, 2)]

    def swap_weights(*weights):
        route = [way for first, second in pairs[1:] for way in ((first, second), (second, first))]
        return tuple(lax.ppermute(weight, "section", route) for weight in weights)

    def embed(found):
        own = lax.cond(section_index == 0, look_up, lambda: found)
        embedded = own + lax.ppermute(own, "section", [(0, half), (half, 0)])
        return only([half], table_project, (embedded, *own_weights), (4,) + part)

    (updated,) = only([0], encode, (patches.reshape(part), *own_weights), part)
    (found,) = lax.cond(section_index != 0, look_up_and_add, lambda: tuple(nothing(part)))
    swapped = lax.cond(
        section_index >= 2,
        swap_weights,
        lambda *_: tuple(nothing(*[weight.shape for weight in own_weights])),
        after(norm_gain, found),
        *own_weights[1:],
    )
    result = updated
    stream = exchange(after(updated, found, *swapped), "section", pairs)
    (table,) = only([0, half], embed, (after(found, stream),), (4,) + part)
    table = lax.cond(
        member(half, half + 1),
        lambda rows: lax.ppermute(rows, "section", [(half, half + 1), (half + 1, half)]),
        lambda rows: nothing(rows.shape)[0],
        table,
    )
    for even in range(0, section_count, 2):
        odd = even + 1
        returned = None
        if even and even < half:
            (updated,) = only([odd], encode, (stream, *swapped), part)
        elif even == half:
            shapes = [part, part, part] + ([whole] if odd + 1 < section_count else [])
            updated, keys, values, *memory = only(
                [odd],
                lambda rows, table: first_decode(rows, table, swapped, own_weights)[: len(shapes)],
                (stream, table),
                *shapes,
            )
        elif even > half:
            keys, values = only([odd], lambda rows: memory_project(rows, swapped), memory, part, part)
            (updated,) = only([odd], decode, (stream, keys, values, *swapped), part)
            keys, values = only(
                [odd], lambda rows: memory_project(rows, own_weights), memory, part, part
            )
        if even:
            returned = exchange(updated, "section", pairs)
            stream = updated
        if even < half:
            (updated,) = only([odd], encode, (stream, *own_weights), part)
        else:
            (updated,) = only([odd], decode, (stream, keys, values, *own_weights), part)
        if returned is not None:
            result = jnp.where(section_index == even, returned, result)
        result = jnp.where(section_index == odd, updated, result)
        if odd + 1 < section_count:
            ahead = [(odd, odd + 2), (even, even + 2)]
            if even >= half:
                memory = [exchange(memory[0], "section", ahead)]
            else:
                updated = after(updated, table)
            stream = exchange(updated, "section", ahead)
    return result.reshape(1, micro_count, row_count, width_local)


def solution(mesh):
    return jax.shard_map(
        local,
        mesh=mesh,
        in_specs=(
            P(None, None, "tp"),
            P(),
            P(),
            P("section", "tp"),
            P("section", None),
            P("section", None, "tp"),
            P("section", None, "tp"),
            P("section", None, "tp"),
            P("section", None, "tp"),
        ),
        out_specs=P("section", None, None, "tp"),
        check_vma=False,
    )
```

```python
import math

import jax
import jax.numpy as jnp
from jax import lax
from jax.experimental import pallas as pl
from jax.sharding import PartitionSpec as P

HEADS = 32


epsilon = 1e-06


def gather_steps(count):
    bits = [1 << i for i in reversed(range(count.bit_length() - 1))]
    steps = []
    while bits:
        if len(bits) % 2:
            steps.append([bits[0]])
            bits = bits[1:]
        else:
            steps.append([bits[0] | bits[1], bits[0], bits[1]])
            bits = bits[2:]
    return steps


def gather_rows(block, axis):
    count = lax.axis_size(axis)
    me = lax.axis_index(axis)
    held = [(block[None], [0])]
    for masks in gather_steps(count):
        if len(held) > 2:
            piece = jnp.concatenate([one for one, _ in held], axis=0)
            held = [(piece, [s for _, sources in held for s in sources])]
        received = []
        for piece, sources in held:
            for mask in masks:
                route = [(i, i ^ mask) for i in range(count)]
                received.append((lax.ppermute(piece, axis, route), [s ^ mask for s in sources]))
        held = held + received
    pieces = {mask: piece[i] for piece, sources in held for i, mask in enumerate(sources)}
    top = count // 2
    swap = (me & top) != 0
    halves = {
        m: jnp.stack(
            [
                jnp.where(swap, pieces[m ^ top], pieces[m]),
                jnp.where(swap, pieces[m], pieces[m ^ top]),
            ]
        )
        for m in range(top)
    }
    bit = top // 2
    while bit:
        swap = (me & bit) != 0
        halves = {m: jnp.where(swap, halves[m ^ bit], halves[m]) for m in halves}
        bit //= 2
    full = jnp.stack([halves[m] for m in range(top)], axis=1)
    full = full.reshape((count,) + block.shape).transpose(1, 0, 2)
    return full.reshape(block.shape[0], count * block.shape[1])


def exchange(block, axis, pairs):
    used = [index for pair in pairs for index in pair]
    rest = [index for index in range(lax.axis_size(axis)) if index not in used]
    pairs = list(pairs) + list(zip(rest[0::2], rest[1::2]))
    route = [way for first, second in pairs for way in ((first, second), (second, first))]
    return lax.ppermute(block, axis, route)


def nothing(*shapes):
    specs = [pl.BlockSpec(memory_space=pl.ANY)] * len(shapes)
    return pl.pallas_call(
        lambda *refs: None,
        out_shape=[jax.ShapeDtypeStruct(shape, jnp.bfloat16) for shape in shapes],
        out_specs=specs,
    )()


def local(patches, table_ids, lengths, embed_table, norm_gain, w_query, w_key, w_value, w_out):
    section_count = lax.axis_size("section")
    section_index = lax.axis_index("section")
    half = section_count // 2
    micro_count, row_count, width_local = patches.shape
    width_full = w_query.shape[1]
    head_dim = width_full // HEADS
    heads_local = width_local // head_dim
    score_scale = 1.0 / math.sqrt(head_dim)
    own_weights = (norm_gain, w_query[0], w_key[0], w_value[0], w_out[0])
    total_rows = micro_count * row_count
    vocab_local = embed_table.shape[0]
    bf16 = jnp.bfloat16
    part = (total_rows, width_local)
    whole = (total_rows, width_full)

    def member(*indices):
        taken = section_index == indices[0]
        for index in indices[1:]:
            taken = taken | (section_index == index)
        return taken

    def only(indices, body, operands, *shapes):
        return lax.cond(member(*indices), body, lambda *_: tuple(nothing(*shapes)), *operands)

    def after(value, *earlier):
        return lax.optimization_barrier((value,) + earlier)[0]

    def look_up():
        local_ids = table_ids.reshape(-1) - section_index * vocab_local
        vocab_cols = lax.broadcasted_iota(jnp.int32, (total_rows, vocab_local), 1)
        one_hot = (local_ids[:, None] == vocab_cols).astype(bf16)
        return jnp.dot(one_hot, embed_table, preferred_element_type=jnp.float32).astype(bf16)

    def look_up_and_add():
        found = look_up()
        others = list(range(1, section_count))
        total = found
        for shift in range(1, len(others)):
            route = [(s, others[(i + shift) % len(others)]) for i, s in enumerate(others)]
            total = total + lax.ppermute(found, "section", route)
        return (total,)

    def normalise(full, gain):
        values_f = full.astype(jnp.float32)
        inverse = lax.rsqrt(jnp.mean(values_f * values_f, axis=-1, keepdims=True) + epsilon)
        return (values_f * inverse * gain.astype(jnp.float32)).astype(bf16)

    def multiply(rows, weight):
        return jnp.dot(rows, weight, preferred_element_type=jnp.float32)

    def project(full, weights):
        gain, query_weight, key_weight, value_weight = weights
        normed = normalise(full, gain)
        return (
            (multiply(normed, query_weight) * score_scale).astype(bf16),
            multiply(normed, key_weight).astype(bf16),
            multiply(normed, value_weight).astype(bf16),
        )

    def heads_of(rows):
        return rows.reshape(micro_count, row_count, heads_local, head_dim)

    def attend(query, keys, values, mask):
        scores = jnp.einsum("mqhd,mkhd->mhqk", query, keys, preferred_element_type=jnp.float32)
        exp_scores = jnp.where(mask[:, None], jnp.exp(scores), 0.0)
        weights = (exp_scores / jnp.sum(exp_scores, axis=-1, keepdims=True)).astype(bf16)
        mix = jnp.einsum("mhqk,mkhd->mqhd", weights, values, preferred_element_type=jnp.float32)
        return mix.astype(bf16).reshape(part)

    mask_shape = (micro_count, row_count, row_count)

    def patch_mask():
        key_pos = lax.broadcasted_iota(jnp.int32, mask_shape, 2)
        return key_pos < lengths[:, 0][:, None, None]

    def encoder_mix(query, keys, values):
        return attend(heads_of(query), heads_of(keys), heads_of(values), patch_mask())

    def decoder_mix(memory_keys, memory_values, query, keys, values):
        query_pos = lax.broadcasted_iota(jnp.int32, mask_shape, 1)
        key_pos = lax.broadcasted_iota(jnp.int32, mask_shape, 2)
        own = (key_pos <= query_pos) & (key_pos < lengths[:, 1][:, None, None])
        return attend(
            heads_of(query),
            jnp.concatenate([heads_of(memory_keys), heads_of(keys)], axis=1),
            jnp.concatenate([heads_of(memory_values), heads_of(values)], axis=1),
            jnp.concatenate([patch_mask(), own], axis=2),
        )

    def finish(stream, mix, out_weight):
        change = multiply(gather_rows(mix, "tp"), out_weight)
        return (stream.astype(jnp.float32) + change).astype(bf16)

    def gather_and_project(stream, *weights):
        return project(gather_rows(stream, "tp"), weights)

    def encoder_end(stream, query, keys, values, out_weight):
        return (finish(stream, encoder_mix(query, keys, values), out_weight),)

    def decoder_end(stream, out_weight, *heads):
        return (finish(stream, decoder_mix(*heads), out_weight),)

    def memory_project(memory, weights):
        gain, _, key_weight, value_weight, _ = weights
        normed = normalise(memory, gain)
        keys, values = multiply(normed, key_weight), multiply(normed, value_weight)
        return keys.astype(bf16), values.astype(bf16)

    def encode(index, stream, weights):
        heads = only([index], gather_and_project, (stream, *weights[:4]), part, part, part)
        return only([index], encoder_end, (stream, *heads, weights[4]), part)[0]

    def decode(index, stream, keys, values, weights):
        heads = only([index], gather_and_project, (stream, *weights[:4]), part, part, part)
        return only([index], decoder_end, (stream, weights[4], keys, values, *heads), part)[0]

    def table_project(stream, *weights):
        return (jnp.stack(gather_and_project(stream, *weights[:4]) + (stream,)),)

    def memory_start(stream, weights, following):
        memory = gather_rows(stream, "tp")
        return (*memory_project(memory, weights), *memory_project(memory, following), memory)

    pairs = [(index, index + 1) for index in range(0, section_count, 2)]

    def swap_weights(*weights):
        route = [way for first, second in pairs[1:] for way in ((first, second), (second, first))]
        return tuple(lax.ppermute(weight, "section", route) for weight in weights)

    def embed(found):
        own = lax.cond(section_index == 0, look_up, lambda: found)
        embedded = own + lax.ppermute(own, "section", [(0, half), (half, 0)])
        return only([half], table_project, (embedded, *own_weights), (4,) + part)

    updated = encode(0, patches.reshape(part), own_weights)
    (found,) = lax.cond(section_index != 0, look_up_and_add, lambda: tuple(nothing(part)))
    swapped = lax.cond(
        section_index >= 2,
        swap_weights,
        lambda *_: tuple(nothing(*[weight.shape for weight in own_weights])),
        after(norm_gain, found),
        *own_weights[1:],
    )
    result = updated
    stream = exchange(after(updated, found, *swapped), "section", pairs)
    (table,) = only([0, half], embed, (after(found, stream),), (4,) + part)
    table = lax.cond(
        member(half, half + 1),
        lambda rows: lax.ppermute(rows, "section", [(half, half + 1), (half + 1, half)]),
        lambda rows: nothing(rows.shape)[0],
        table,
    )
    for even in range(0, section_count, 2):
        odd = even + 1
        returned = None
        if even and even < half:
            updated = encode(odd, stream, swapped)
        elif even == half:
            shapes = [part] * 4 + ([whole] if odd + 1 < section_count else [])
            first_keys, first_values, keys, values, *memory = only(
                [odd],
                lambda rows: memory_start(rows, swapped, own_weights)[: len(shapes)],
                (stream,),
                *shapes,
            )
            (updated,) = only(
                [odd],
                lambda rows, *rest: decoder_end(rows[3], *rest, rows[0], rows[1], rows[2]),
                (table, swapped[4], first_keys, first_values),
                part,
            )
        elif even > half:
            keys, values = only([odd], lambda rows: memory_project(rows, swapped), memory, part, part)
            updated = decode(odd, stream, keys, values, swapped)
            keys, values = only(
                [odd], lambda rows: memory_project(rows, own_weights), memory, part, part
            )
        if even:
            returned = exchange(updated, "section", pairs)
            stream = updated
        if even < half:
            updated = encode(odd, stream, own_weights)
        else:
            updated = decode(odd, stream, keys, values, own_weights)
        if returned is not None:
            result = jnp.where(section_index == even, returned, result)
        result = jnp.where(section_index == odd, updated, result)
        if odd + 1 < section_count:
            ahead = [(odd, odd + 2), (even, even + 2)]
            if even >= half:
                memory = [exchange(memory[0], "section", ahead)]
            else:
                updated = after(updated, table)
            stream = exchange(updated, "section", ahead)
    return result.reshape(1, micro_count, row_count, width_local)


def solution(mesh):
    return jax.shard_map(
        local,
        mesh=mesh,
        in_specs=(
            P(None, None, "tp"),
            P(),
            P(),
            P("section", "tp"),
            P("section", None),
            P("section", None, "tp"),
            P("section", None, "tp"),
            P("section", None, "tp"),
            P("section", None, "tp"),
        ),
        out_specs=P("section", None, None, "tp"),
        check_vma=False,
    )
```

```python
import functools
import math

import jax
import jax.numpy as jnp
from jax import lax
from jax.experimental import pallas as pl
from jax.experimental.pallas import tpu as pltpu
from jax.sharding import PartitionSpec as P

HEADS = 32


epsilon = 1e-06


CHUNKS = 4


def load_kernel(weight_ref, _, out_ref, sems):
    rows = weight_ref.shape[0] // CHUNKS
    copies = []
    for i in range(CHUNKS):
        part = pl.ds(i * rows, rows)
        copies.append(pltpu.make_async_copy(weight_ref.at[part], out_ref.at[part], sems.at[i]))
    for copy in copies:
        copy.start()
    for copy in copies:
        copy.wait()


def load(weight, moment):
    return pl.pallas_call(
        load_kernel,
        out_shape=pltpu.VMEM(weight.shape, weight.dtype),
        in_specs=[pl.BlockSpec(memory_space=pl.ANY)] * 2,
        out_specs=pl.BlockSpec(memory_space=pltpu.VMEM),
        scratch_shapes=[pltpu.SemaphoreType.DMA((CHUNKS,))],
        compiler_params=pltpu.CompilerParams(vmem_limit_bytes=1 << 20),
        cost_estimate=pl.CostEstimate(
            flops=0, bytes_accessed=4 * weight.size, transcendentals=0
        ),
    )(weight, moment)


def gather_steps(count):
    bits = [1 << i for i in reversed(range(count.bit_length() - 1))]
    steps = []
    while bits:
        if len(bits) % 2:
            steps.append([bits[0]])
            bits = bits[1:]
        else:
            steps.append([bits[0] | bits[1], bits[0], bits[1]])
            bits = bits[2:]
    return steps


def gather_rows(block, axis, weights=()):
    count = lax.axis_size(axis)
    me = lax.axis_index(axis)
    held = [(block[None], [0])]
    for masks in gather_steps(count):
        if len(held) > 2:
            piece = jnp.concatenate([one for one, _ in held], axis=0)
            held = [(piece, [s for _, sources in held for s in sources])]
        received = []
        for piece, sources in held:
            for mask in masks:
                route = [(i, i ^ mask) for i in range(count)]
                received.append((lax.ppermute(piece, axis, route), [s ^ mask for s in sources]))
        held = held + received
    loaded = [load(weight, held[1][0]) for weight in weights]
    pieces = {mask: piece[i] for piece, sources in held for i, mask in enumerate(sources)}
    top = count // 2
    swap = (me & top) != 0
    halves = {
        m: jnp.stack(
            [
                jnp.where(swap, pieces[m ^ top], pieces[m]),
                jnp.where(swap, pieces[m], pieces[m ^ top]),
            ]
        )
        for m in range(top)
    }
    bit = top // 2
    while bit:
        swap = (me & bit) != 0
        halves = {m: jnp.where(swap, halves[m ^ bit], halves[m]) for m in halves}
        bit //= 2
    full = jnp.stack([halves[m] for m in range(top)], axis=1)
    full = full.reshape((count,) + block.shape).transpose(1, 0, 2)
    full = full.reshape(block.shape[0], count * block.shape[1])
    return (full, *loaded) if weights else full


def exchange(block, axis, pairs):
    used = [index for pair in pairs for index in pair]
    rest = [index for index in range(lax.axis_size(axis)) if index not in used]
    pairs = list(pairs) + list(zip(rest[0::2], rest[1::2]))
    route = [way for first, second in pairs for way in ((first, second), (second, first))]
    return lax.ppermute(block, axis, route)


def nothing(*shapes):
    specs = [pl.BlockSpec(memory_space=pl.ANY)] * len(shapes)
    return pl.pallas_call(
        lambda *refs: None,
        out_shape=[jax.ShapeDtypeStruct(shape, jnp.bfloat16) for shape in shapes],
        out_specs=specs,
    )()


def local(patches, table_ids, lengths, embed_table, norm_gain, w_query, w_key, w_value, w_out):
    section_count = lax.axis_size("section")
    section_index = lax.axis_index("section")
    half = section_count // 2
    micro_count, row_count, width_local = patches.shape
    width_full = w_query.shape[1]
    head_dim = width_full // HEADS
    heads_local = width_local // head_dim
    score_scale = 1.0 / math.sqrt(head_dim)
    own_weights = (norm_gain, w_query[0], w_key[0], w_value[0], w_out[0])
    total_rows = micro_count * row_count
    vocab_local = embed_table.shape[0]
    bf16 = jnp.bfloat16
    part = (total_rows, width_local)
    whole = (total_rows, width_full)

    def member(*indices):
        taken = section_index == indices[0]
        for index in indices[1:]:
            taken = taken | (section_index == index)
        return taken

    def only(indices, body, operands, *shapes):
        return lax.cond(member(*indices), body, lambda *_: tuple(nothing(*shapes)), *operands)

    def after(value, *earlier):
        return lax.optimization_barrier((value,) + earlier)[0]

    def look_up():
        local_ids = table_ids.reshape(-1) - section_index * vocab_local
        vocab_cols = lax.broadcasted_iota(jnp.int32, (total_rows, vocab_local), 1)
        one_hot = (local_ids[:, None] == vocab_cols).astype(bf16)
        return jnp.dot(one_hot, embed_table, preferred_element_type=jnp.float32).astype(bf16)

    def look_up_and_add():
        found = look_up()
        others = list(range(1, section_count))
        total = found
        for shift in range(1, len(others)):
            route = [(s, others[(i + shift) % len(others)]) for i, s in enumerate(others)]
            total = total + lax.ppermute(found, "section", route)
        return (total,)

    def normalise(full, gain):
        values_f = full.astype(jnp.float32)
        inverse = lax.rsqrt(jnp.mean(values_f * values_f, axis=-1, keepdims=True) + epsilon)
        return (values_f * inverse * gain.astype(jnp.float32)).astype(bf16)

    def multiply(rows, weight):
        return jnp.dot(rows, weight, preferred_element_type=jnp.float32)

    def project(full, weights):
        gain, query_weight, key_weight, value_weight = weights
        normed = normalise(full, gain)
        return (
            (multiply(normed, query_weight) * score_scale).astype(bf16),
            multiply(normed, key_weight).astype(bf16),
            multiply(normed, value_weight).astype(bf16),
        )

    def heads_of(rows):
        return rows.reshape(micro_count, row_count, heads_local, head_dim)

    def attend(query, keys, values, mask):
        scores = jnp.einsum("mqhd,mkhd->mhqk", query, keys, preferred_element_type=jnp.float32)
        exp_scores = jnp.where(mask[:, None], jnp.exp(scores), 0.0)
        weights = (exp_scores / jnp.sum(exp_scores, axis=-1, keepdims=True)).astype(bf16)
        mix = jnp.einsum("mhqk,mkhd->mqhd", weights, values, preferred_element_type=jnp.float32)
        return mix.astype(bf16).reshape(part)

    mask_shape = (micro_count, row_count, row_count)

    def patch_mask():
        key_pos = lax.broadcasted_iota(jnp.int32, mask_shape, 2)
        return key_pos < lengths[:, 0][:, None, None]

    def encoder_mix(query, keys, values):
        return attend(heads_of(query), heads_of(keys), heads_of(values), patch_mask())

    def decoder_mix(memory_keys, memory_values, query, keys, values):
        query_pos = lax.broadcasted_iota(jnp.int32, mask_shape, 1)
        key_pos = lax.broadcasted_iota(jnp.int32, mask_shape, 2)
        own = (key_pos <= query_pos) & (key_pos < lengths[:, 1][:, None, None])
        return attend(
            heads_of(query),
            jnp.concatenate([heads_of(memory_keys), heads_of(keys)], axis=1),
            jnp.concatenate([heads_of(memory_values), heads_of(values)], axis=1),
            jnp.concatenate([patch_mask(), own], axis=2),
        )

    def finish(stream, mix, out_weight, shipped=False):
        if shipped:
            full, out_weight = gather_rows(mix, "tp", (out_weight,))
        else:
            full = gather_rows(mix, "tp")
        change = multiply(full, out_weight)
        return (stream.astype(jnp.float32) + change).astype(bf16)

    def gather_and_project(stream, *weights):
        return project(gather_rows(stream, "tp"), weights)

    def encoder_end(stream, query, keys, values, out_weight):
        return (finish(stream, encoder_mix(query, keys, values), out_weight),)

    def decoder_end(stream, out_weight, *heads, shipped=False):
        return (finish(stream, decoder_mix(*heads), out_weight, shipped),)

    def memory_project(stream, gain, key_weight, value_weight):
        memory, key_weight, value_weight = gather_rows(
            stream, "tp", (key_weight, value_weight)
        )
        normed = normalise(memory, gain)
        keys, values = multiply(normed, key_weight), multiply(normed, value_weight)
        return keys.astype(bf16), values.astype(bf16), memory

    def both_project(stream, memory, gain, query_weight, key_weight, value_weight):
        normed = normalise(gather_rows(stream, "tp"), gain)
        rows = jnp.concatenate([normalise(memory, gain), normed], axis=0)
        query = (multiply(normed, query_weight) * score_scale).astype(bf16)
        keys = multiply(rows, key_weight).astype(bf16)
        values = multiply(rows, value_weight).astype(bf16)
        return (
            keys[:total_rows],
            values[:total_rows],
            query,
            keys[total_rows:],
            values[total_rows:],
        )

    def encode(index, stream, weights):
        heads = only([index], gather_and_project, (stream, *weights[:4]), part, part, part)
        return only([index], encoder_end, (stream, *heads, weights[4]), part)[0]

    def decode(index, stream, memory, weights, earlier=()):
        heads = only([index], both_project, (stream, memory, *weights[:4]), *[part] * 5)
        heads = lax.optimization_barrier((*heads, earlier))[:5]
        return only([index], decoder_end, (stream, weights[4], *heads), part)[0]

    def table_project(stream, *weights):
        return (jnp.stack(gather_and_project(stream, *weights[:4]) + (stream,)),)

    pairs = [(index, index + 1) for index in range(0, section_count, 2)]

    def swap_weights(*weights):
        route = [way for first, second in pairs[1:] for way in ((first, second), (second, first))]
        return tuple(lax.ppermute(weight, "section", route) for weight in weights)

    def embed(found):
        own = lax.cond(section_index == 0, look_up, lambda: found)
        embedded = own + lax.ppermute(own, "section", [(0, half), (half, 0)])
        return only([half], table_project, (embedded, *own_weights), (4,) + part)

    updated = encode(0, patches.reshape(part), own_weights)
    (found,) = lax.cond(section_index != 0, look_up_and_add, lambda: tuple(nothing(part)))
    swapped = lax.cond(
        section_index >= 2,
        swap_weights,
        lambda *_: tuple(nothing(*[weight.shape for weight in own_weights])),
        after(norm_gain, found),
        *own_weights[1:],
    )
    result = updated
    stream = exchange(after(updated, found, *swapped), "section", pairs)
    (table,) = only([0, half], embed, (after(found, stream),), (4,) + part)
    for even in range(0, section_count, 2):
        odd = even + 1
        returned = None
        if even and even < half:
            updated = encode(odd, stream, swapped)
        elif even == half:
            gain, _, key_weight, value_weight, out_weight = swapped
            first_keys, first_values, memory = only(
                [odd], memory_project, (stream, gain, key_weight, value_weight), part, part, whole
            )
            table = exchange(after(table, first_keys), "section", pairs)
            (updated,) = only(
                [odd],
                functools.partial(decoder_end, shipped=True),
                (table[3], out_weight, first_keys, first_values, *table[:3]),
                part,
            )
        elif even > half:
            updated = decode(odd, stream, memory, swapped)
        if even:
            returned = exchange(updated, "section", pairs)
            stream = updated
        if even < half:
            updated = encode(odd, stream, own_weights)
        else:
            updated = decode(odd, stream, memory, own_weights, (returned,))
        if returned is not None:
            result = jnp.where(section_index == even, returned, result)
        result = jnp.where(section_index == odd, updated, result)
        if odd + 1 < section_count:
            ahead = [(odd, odd + 2), (even, even + 2)]
            if even >= half:
                memory = exchange(memory, "section", ahead)
            else:
                updated = after(updated, found)
            stream = exchange(updated, "section", ahead)
    return result.reshape(1, micro_count, row_count, width_local)


def solution(mesh):
    return jax.shard_map(
        local,
        mesh=mesh,
        in_specs=(
            P(None, None, "tp"),
            P(),
            P(),
            P("section", "tp"),
            P("section", None),
            P("section", None, "tp"),
            P("section", None, "tp"),
            P("section", None, "tp"),
            P("section", None, "tp"),
        ),
        out_specs=P("section", None, None, "tp"),
        check_vma=False,
    )
```

```python
import functools
import math

import jax
import jax.numpy as jnp
from jax import lax
from jax.experimental import pallas as pl
from jax.experimental.pallas import tpu as pltpu
from jax.sharding import PartitionSpec as P

HEADS = 32


epsilon = 1e-06


CHUNKS = 4


def load_kernel(weight_ref, _, out_ref, sems):
    rows = weight_ref.shape[0] // CHUNKS
    copies = []
    for i in range(CHUNKS):
        part = pl.ds(i * rows, rows)
        copies.append(pltpu.make_async_copy(weight_ref.at[part], out_ref.at[part], sems.at[i]))
    for copy in copies:
        copy.start()
    for copy in copies:
        copy.wait()


def load(weight, moment):
    return pl.pallas_call(
        load_kernel,
        out_shape=pltpu.VMEM(weight.shape, weight.dtype),
        in_specs=[pl.BlockSpec(memory_space=pl.ANY)] * 2,
        out_specs=pl.BlockSpec(memory_space=pltpu.VMEM),
        scratch_shapes=[pltpu.SemaphoreType.DMA((CHUNKS,))],
        compiler_params=pltpu.CompilerParams(vmem_limit_bytes=1 << 20),
        cost_estimate=pl.CostEstimate(
            flops=0, bytes_accessed=4 * weight.size, transcendentals=0
        ),
    )(weight, moment)


def gather_steps(count):
    bits = [1 << i for i in reversed(range(count.bit_length() - 1))]
    steps = []
    while bits:
        if len(bits) % 2:
            steps.append([bits[0]])
            bits = bits[1:]
        else:
            steps.append([bits[0] | bits[1], bits[0], bits[1]])
            bits = bits[2:]
    return steps


def gather_rows(block, axis, weights=()):
    count = lax.axis_size(axis)
    me = lax.axis_index(axis)
    held = [(block[None], [0])]
    for masks in gather_steps(count):
        if len(held) > 2:
            piece = jnp.concatenate([one for one, _ in held], axis=0)
            held = [(piece, [s for _, sources in held for s in sources])]
        received = []
        for piece, sources in held:
            for mask in masks:
                route = [(i, i ^ mask) for i in range(count)]
                received.append((lax.ppermute(piece, axis, route), [s ^ mask for s in sources]))
        held = held + received
    loaded = [load(weight, held[1][0]) for weight in weights]
    pieces = {mask: piece[i] for piece, sources in held for i, mask in enumerate(sources)}
    top = count // 2
    swap = (me & top) != 0
    halves = {
        m: jnp.stack(
            [
                jnp.where(swap, pieces[m ^ top], pieces[m]),
                jnp.where(swap, pieces[m], pieces[m ^ top]),
            ]
        )
        for m in range(top)
    }
    bit = top // 2
    while bit:
        swap = (me & bit) != 0
        halves = {m: jnp.where(swap, halves[m ^ bit], halves[m]) for m in halves}
        bit //= 2
    full = jnp.stack([halves[m] for m in range(top)], axis=1)
    full = full.reshape((count,) + block.shape).transpose(1, 0, 2)
    full = full.reshape(block.shape[0], count * block.shape[1])
    return (full, *loaded) if weights else full


def exchange(block, axis, pairs):
    used = [index for pair in pairs for index in pair]
    rest = [index for index in range(lax.axis_size(axis)) if index not in used]
    pairs = list(pairs) + list(zip(rest[0::2], rest[1::2]))
    route = [way for first, second in pairs for way in ((first, second), (second, first))]
    return lax.ppermute(block, axis, route)


def nothing(*shapes):
    specs = [pl.BlockSpec(memory_space=pl.ANY)] * len(shapes)
    return pl.pallas_call(
        lambda *refs: None,
        out_shape=[jax.ShapeDtypeStruct(shape, jnp.bfloat16) for shape in shapes],
        out_specs=specs,
    )()


def local(patches, table_ids, lengths, embed_table, norm_gain, w_query, w_key, w_value, w_out):
    section_count = lax.axis_size("section")
    section_index = lax.axis_index("section")
    half = section_count // 2
    micro_count, row_count, width_local = patches.shape
    width_full = w_query.shape[1]
    head_dim = width_full // HEADS
    heads_local = width_local // head_dim
    score_scale = 1.0 / math.sqrt(head_dim)
    own_weights = (norm_gain, w_query[0], w_key[0], w_value[0], w_out[0])
    total_rows = micro_count * row_count
    vocab_local = embed_table.shape[0]
    bf16 = jnp.bfloat16
    part = (total_rows, width_local)
    whole = (total_rows, width_full)

    def member(*indices):
        taken = section_index == indices[0]
        for index in indices[1:]:
            taken = taken | (section_index == index)
        return taken

    def only(indices, body, operands, *shapes):
        return lax.cond(member(*indices), body, lambda *_: tuple(nothing(*shapes)), *operands)

    def after(value, *earlier):
        return lax.optimization_barrier((value,) + earlier)[0]

    def look_up():
        local_ids = table_ids.reshape(-1) - section_index * vocab_local
        vocab_cols = lax.broadcasted_iota(jnp.int32, (total_rows, vocab_local), 1)
        one_hot = (local_ids[:, None] == vocab_cols).astype(bf16)
        return jnp.dot(one_hot, embed_table, preferred_element_type=jnp.float32).astype(bf16)

    def look_up_and_add():
        found = look_up()
        others = list(range(1, section_count))
        total = found
        for shift in range(1, len(others)):
            route = [(s, others[(i + shift) % len(others)]) for i, s in enumerate(others)]
            total = total + lax.ppermute(found, "section", route)
        return (total,)

    def normalise(full, gain):
        values_f = full.astype(jnp.float32)
        inverse = lax.rsqrt(jnp.mean(values_f * values_f, axis=-1, keepdims=True) + epsilon)
        return (values_f * inverse * gain.astype(jnp.float32)).astype(bf16)

    def multiply(rows, weight):
        return jnp.dot(rows, weight, preferred_element_type=jnp.float32)

    def project(full, weights):
        gain, query_weight, key_weight, value_weight = weights
        normed = normalise(full, gain)
        return (
            (multiply(normed, query_weight) * score_scale).astype(bf16),
            multiply(normed, key_weight).astype(bf16),
            multiply(normed, value_weight).astype(bf16),
        )

    def heads_of(rows):
        return rows.reshape(micro_count, row_count, heads_local, head_dim)

    def attend(query, keys, values, mask):
        scores = jnp.einsum("mqhd,mkhd->mhqk", query, keys, preferred_element_type=jnp.float32)
        exp_scores = jnp.where(mask[:, None], jnp.exp(scores), 0.0)
        weights = (exp_scores / jnp.sum(exp_scores, axis=-1, keepdims=True)).astype(bf16)
        mix = jnp.einsum("mhqk,mkhd->mqhd", weights, values, preferred_element_type=jnp.float32)
        return mix.astype(bf16).reshape(part)

    mask_shape = (micro_count, row_count, row_count)

    def patch_mask():
        key_pos = lax.broadcasted_iota(jnp.int32, mask_shape, 2)
        return key_pos < lengths[:, 0][:, None, None]

    def encoder_mix(query, keys, values):
        return attend(heads_of(query), heads_of(keys), heads_of(values), patch_mask())

    def decoder_mix(memory_keys, memory_values, query, keys, values):
        query_pos = lax.broadcasted_iota(jnp.int32, mask_shape, 1)
        key_pos = lax.broadcasted_iota(jnp.int32, mask_shape, 2)
        own = (key_pos <= query_pos) & (key_pos < lengths[:, 1][:, None, None])
        return attend(
            heads_of(query),
            jnp.concatenate([heads_of(memory_keys), heads_of(keys)], axis=1),
            jnp.concatenate([heads_of(memory_values), heads_of(values)], axis=1),
            jnp.concatenate([patch_mask(), own], axis=2),
        )

    def finish(stream, mix, out_weight, shipped=False):
        if shipped:
            full, out_weight = gather_rows(mix, "tp", (out_weight,))
        else:
            full = gather_rows(mix, "tp")
        change = multiply(full, out_weight)
        return (stream.astype(jnp.float32) + change).astype(bf16)

    def gather_and_project(stream, gain, query_weight, key_weight, value_weight):
        full, *loaded = gather_rows(stream, "tp", (key_weight, value_weight))
        return project(full, (gain, query_weight, *loaded))

    def encoder_end(stream, query, keys, values, out_weight):
        return (finish(stream, encoder_mix(query, keys, values), out_weight),)

    def decoder_end(stream, out_weight, *heads, shipped=False):
        return (finish(stream, decoder_mix(*heads), out_weight, shipped),)

    def memory_project(memory, gain, key_weight, value_weight):
        normed = normalise(memory, gain)
        keys, values = multiply(normed, key_weight), multiply(normed, value_weight)
        return keys.astype(bf16), values.astype(bf16)

    def memory_start(stream, gain, key_weight, value_weight, *following):
        memory, *shipped = gather_rows(stream, "tp", (key_weight, value_weight))
        first = memory_project(memory, gain, *shipped)
        return (*first, *memory_project(memory, *following), memory)

    def encode(index, stream, weights):
        heads = only([index], gather_and_project, (stream, *weights[:4]), part, part, part)
        return only([index], encoder_end, (stream, *heads, weights[4]), part)[0]

    def decode(index, stream, keys, values, weights, earlier=()):
        heads = only([index], gather_and_project, (stream, *weights[:4]), part, part, part)
        heads = lax.optimization_barrier((*heads, earlier))[:3]
        return only([index], decoder_end, (stream, weights[4], keys, values, *heads), part)[0]

    def memory_rows(index, memory, weights):
        gain, _, key_weight, value_weight, _ = weights
        operands = (memory, gain, key_weight, value_weight)
        return only([index], memory_project, operands, part, part)

    def table_project(stream, *weights):
        return (jnp.stack(gather_and_project(stream, *weights[:4]) + (stream,)),)

    pairs = [(index, index + 1) for index in range(0, section_count, 2)]

    def swap_weights(*weights):
        route = [way for first, second in pairs[1:] for way in ((first, second), (second, first))]
        return tuple(lax.ppermute(weight, "section", route) for weight in weights)

    def embed(found):
        own = lax.cond(section_index == 0, look_up, lambda: found)
        embedded = own + lax.ppermute(own, "section", [(0, half), (half, 0)])
        return only([half], table_project, (embedded, *own_weights), (4,) + part)

    updated = encode(0, patches.reshape(part), own_weights)
    (found,) = lax.cond(section_index != 0, look_up_and_add, lambda: tuple(nothing(part)))
    swapped = lax.cond(
        section_index >= 2,
        swap_weights,
        lambda *_: tuple(nothing(*[weight.shape for weight in own_weights])),
        after(norm_gain, found),
        *own_weights[1:],
    )
    result = updated
    stream = exchange(after(updated, found, *swapped), "section", pairs)
    (table,) = only([0, half], embed, (after(found, stream),), (4,) + part)
    for even in range(0, section_count, 2):
        odd = even + 1
        returned = None
        if even and even < half:
            updated = encode(odd, stream, swapped)
        elif even == half:
            gain, _, key_weight, value_weight, out_weight = swapped
            shapes = [part] * 4 + ([whole] if odd + 1 < section_count else [])
            first_keys, first_values, keys, values, *memory = only(
                [odd],
                lambda *operands: memory_start(*operands)[: len(shapes)],
                (stream, gain, key_weight, value_weight, norm_gain, w_key[0], w_value[0]),
                *shapes,
            )
            table = exchange(after(table, first_keys), "section", pairs)
            (updated,) = only(
                [odd],
                functools.partial(decoder_end, shipped=True),
                (table[3], out_weight, first_keys, first_values, *table[:3]),
                part,
            )
        elif even > half:
            keys, values = memory_rows(odd, memory[0], swapped)
            updated = decode(odd, stream, keys, values, swapped)
            keys, values = memory_rows(odd, memory[0], own_weights)
        if even:
            returned = exchange(updated, "section", pairs)
            stream = updated
        if even < half:
            updated = encode(odd, stream, own_weights)
        else:
            updated = decode(odd, stream, keys, values, own_weights, (returned,))
        if returned is not None:
            result = jnp.where(section_index == even, returned, result)
        result = jnp.where(section_index == odd, updated, result)
        if odd + 1 < section_count:
            ahead = [(odd, odd + 2), (even, even + 2)]
            if even >= half:
                memory = [exchange(memory[0], "section", ahead)]
            else:
                updated = after(updated, found)
            stream = exchange(updated, "section", ahead)
    return result.reshape(1, micro_count, row_count, width_local)


def solution(mesh):
    return jax.shard_map(
        local,
        mesh=mesh,
        in_specs=(
            P(None, None, "tp"),
            P(),
            P(),
            P("section", "tp"),
            P("section", None),
            P("section", None, "tp"),
            P("section", None, "tp"),
            P("section", None, "tp"),
            P("section", None, "tp"),
        ),
        out_specs=P("section", None, None, "tp"),
        check_vma=False,
    )
```

```python
import functools
import math

import jax
import jax.numpy as jnp
from jax import lax
from jax.experimental import pallas as pl
from jax.experimental.pallas import tpu as pltpu
from jax.sharding import PartitionSpec as P

HEADS = 32


epsilon = 1e-06


CHUNKS = 4


def load_kernel(*refs):
    *refs, sems = refs
    count = len(refs) // 2
    copies = []
    for i, (weight_ref, out_ref) in enumerate(zip(refs[:count], refs[count + 1 :])):
        rows = weight_ref.shape[0] // CHUNKS
        for j in range(CHUNKS):
            part = pl.ds(j * rows, rows)
            copies.append(
                pltpu.make_async_copy(weight_ref.at[part], out_ref.at[part], sems.at[i, j])
            )
    for copy in copies:
        copy.start()
    for copy in copies:
        copy.wait()


def load(weights, moment):
    count = len(weights)
    size = sum(weight.size for weight in weights)
    return pl.pallas_call(
        load_kernel,
        out_shape=[pltpu.VMEM(weight.shape, weight.dtype) for weight in weights],
        in_specs=[pl.BlockSpec(memory_space=pl.ANY)] * (count + 1),
        out_specs=[pl.BlockSpec(memory_space=pltpu.VMEM)] * count,
        scratch_shapes=[pltpu.SemaphoreType.DMA((count, CHUNKS))],
        compiler_params=pltpu.CompilerParams(vmem_limit_bytes=1 << 20),
        cost_estimate=pl.CostEstimate(flops=0, bytes_accessed=4 * size, transcendentals=0),
    )(*weights, moment)


def gather_steps(count):
    bits = [1 << i for i in reversed(range(count.bit_length() - 1))]
    steps = []
    while bits:
        if len(bits) % 2:
            steps.append([bits[0]])
            bits = bits[1:]
        else:
            steps.append([bits[0] | bits[1], bits[0], bits[1]])
            bits = bits[2:]
    return steps


def gather_rows(block, axis, weights=()):
    count = lax.axis_size(axis)
    me = lax.axis_index(axis)
    held = [(block[None], [0])]
    for masks in gather_steps(count):
        if len(held) > 2:
            piece = jnp.concatenate([one for one, _ in held], axis=0)
            held = [(piece, [s for _, sources in held for s in sources])]
        received = []
        for piece, sources in held:
            for mask in masks:
                route = [(i, i ^ mask) for i in range(count)]
                received.append((lax.ppermute(piece, axis, route), [s ^ mask for s in sources]))
        held = held + received
    loaded = load(weights, held[1][0]) if weights else ()
    pieces = {mask: piece[i] for piece, sources in held for i, mask in enumerate(sources)}
    top = count // 2
    swap = (me & top) != 0
    halves = {
        m: jnp.stack(
            [
                jnp.where(swap, pieces[m ^ top], pieces[m]),
                jnp.where(swap, pieces[m], pieces[m ^ top]),
            ]
        )
        for m in range(top)
    }
    bit = top // 2
    while bit:
        swap = (me & bit) != 0
        halves = {m: jnp.where(swap, halves[m ^ bit], halves[m]) for m in halves}
        bit //= 2
    full = jnp.stack([halves[m] for m in range(top)], axis=1)
    full = full.reshape((count,) + block.shape).transpose(1, 0, 2)
    full = full.reshape(block.shape[0], count * block.shape[1])
    return (full, *loaded) if weights else full


def exchange(block, axis, pairs):
    used = [index for pair in pairs for index in pair]
    rest = [index for index in range(lax.axis_size(axis)) if index not in used]
    pairs = list(pairs) + list(zip(rest[0::2], rest[1::2]))
    route = [way for first, second in pairs for way in ((first, second), (second, first))]
    return lax.ppermute(block, axis, route)


def nothing(*shapes):
    specs = [pl.BlockSpec(memory_space=pl.ANY)] * len(shapes)
    return pl.pallas_call(
        lambda *refs: None,
        out_shape=[jax.ShapeDtypeStruct(shape, jnp.bfloat16) for shape in shapes],
        out_specs=specs,
    )()


def local(patches, table_ids, lengths, embed_table, norm_gain, w_query, w_key, w_value, w_out):
    section_count = lax.axis_size("section")
    section_index = lax.axis_index("section")
    half = section_count // 2
    micro_count, row_count, width_local = patches.shape
    width_full = w_query.shape[1]
    head_dim = width_full // HEADS
    heads_local = width_local // head_dim
    score_scale = 1.0 / math.sqrt(head_dim)
    own_weights = (norm_gain, w_query[0], w_key[0], w_value[0], w_out[0])
    total_rows = micro_count * row_count
    vocab_local = embed_table.shape[0]
    bf16 = jnp.bfloat16
    part = (total_rows, width_local)
    whole = (total_rows, width_full)

    def member(*indices):
        taken = section_index == indices[0]
        for index in indices[1:]:
            taken = taken | (section_index == index)
        return taken

    def only(indices, body, operands, *shapes):
        return lax.cond(member(*indices), body, lambda *_: tuple(nothing(*shapes)), *operands)

    def after(value, *earlier):
        return lax.optimization_barrier((value,) + earlier)[0]

    def look_up():
        local_ids = table_ids.reshape(-1) - section_index * vocab_local
        vocab_cols = lax.broadcasted_iota(jnp.int32, (total_rows, vocab_local), 1)
        one_hot = (local_ids[:, None] == vocab_cols).astype(bf16)
        return jnp.dot(one_hot, embed_table, preferred_element_type=jnp.float32).astype(bf16)

    def look_up_and_add():
        found = look_up()
        others = list(range(1, section_count))
        total = found
        for shift in range(1, len(others)):
            route = [(s, others[(i + shift) % len(others)]) for i, s in enumerate(others)]
            total = total + lax.ppermute(found, "section", route)
        return (total,)

    def normalise(full, gain):
        values_f = full.astype(jnp.float32)
        inverse = lax.rsqrt(jnp.mean(values_f * values_f, axis=-1, keepdims=True) + epsilon)
        return (values_f * inverse * gain.astype(jnp.float32)).astype(bf16)

    def multiply(rows, weight):
        return jnp.dot(rows, weight, preferred_element_type=jnp.float32)

    def project(full, weights):
        gain, query_weight, key_weight, value_weight = weights
        normed = normalise(full, gain)
        return (
            (multiply(normed, query_weight) * score_scale).astype(bf16),
            multiply(normed, key_weight).astype(bf16),
            multiply(normed, value_weight).astype(bf16),
        )

    def heads_of(rows):
        return rows.reshape(micro_count, row_count, heads_local, head_dim)

    def attend(query, keys, values, mask):
        scores = jnp.einsum("mqhd,mkhd->mhqk", query, keys, preferred_element_type=jnp.float32)
        exp_scores = jnp.where(mask[:, None], jnp.exp(scores), 0.0)
        weights = (exp_scores / jnp.sum(exp_scores, axis=-1, keepdims=True)).astype(bf16)
        mix = jnp.einsum("mhqk,mkhd->mqhd", weights, values, preferred_element_type=jnp.float32)
        return mix.astype(bf16).reshape(part)

    mask_shape = (micro_count, row_count, row_count)

    def patch_mask():
        key_pos = lax.broadcasted_iota(jnp.int32, mask_shape, 2)
        return key_pos < lengths[:, 0][:, None, None]

    def encoder_mix(query, keys, values):
        return attend(heads_of(query), heads_of(keys), heads_of(values), patch_mask())

    def decoder_mix(memory_keys, memory_values, query, keys, values):
        query_pos = lax.broadcasted_iota(jnp.int32, mask_shape, 1)
        key_pos = lax.broadcasted_iota(jnp.int32, mask_shape, 2)
        own = (key_pos <= query_pos) & (key_pos < lengths[:, 1][:, None, None])
        return attend(
            heads_of(query),
            jnp.concatenate([heads_of(memory_keys), heads_of(keys)], axis=1),
            jnp.concatenate([heads_of(memory_values), heads_of(values)], axis=1),
            jnp.concatenate([patch_mask(), own], axis=2),
        )

    def finish(stream, mix, out_weight, shipped=False):
        if shipped:
            full, out_weight = gather_rows(mix, "tp", (out_weight,))
        else:
            full = gather_rows(mix, "tp")
        change = multiply(full, out_weight)
        return (stream.astype(jnp.float32) + change).astype(bf16)

    def gather_and_project(stream, gain, query_weight, key_weight, value_weight):
        full, *loaded = gather_rows(stream, "tp", (key_weight, value_weight))
        return project(full, (gain, query_weight, *loaded))

    def encoder_end(stream, query, keys, values, out_weight):
        return (finish(stream, encoder_mix(query, keys, values), out_weight),)

    def decoder_end(stream, out_weight, *heads, shipped=False):
        return (finish(stream, decoder_mix(*heads), out_weight, shipped),)

    def memory_project(memory, gain, key_weight, value_weight):
        normed = normalise(memory, gain)
        keys, values = multiply(normed, key_weight), multiply(normed, value_weight)
        return keys.astype(bf16), values.astype(bf16)

    def memory_start(stream, gain, key_weight, value_weight, *following):
        memory, *shipped = gather_rows(stream, "tp", (key_weight, value_weight))
        first = memory_project(memory, gain, *shipped)
        memory = after(memory, *first)
        return (*first, *memory_project(memory, *following), memory)

    def encode(index, stream, weights):
        heads = only([index], gather_and_project, (stream, *weights[:4]), part, part, part)
        return only([index], encoder_end, (stream, *heads, weights[4]), part)[0]

    def decode(index, stream, keys, values, weights, earlier=()):
        heads = only([index], gather_and_project, (stream, *weights[:4]), part, part, part)
        heads = lax.optimization_barrier((*heads, earlier))[:3]
        return only([index], decoder_end, (stream, weights[4], keys, values, *heads), part)[0]

    def memory_rows(index, memory, weights):
        gain, _, key_weight, value_weight, _ = weights
        operands = (memory, gain, key_weight, value_weight)
        return only([index], memory_project, operands, part, part)

    def table_project(stream, *weights):
        return (jnp.stack(gather_and_project(stream, *weights[:4]) + (stream,)),)

    pairs = [(index, index + 1) for index in range(0, section_count, 2)]

    def swap_weights(*weights):
        route = [way for first, second in pairs[1:] for way in ((first, second), (second, first))]
        return tuple(lax.ppermute(weight, "section", route) for weight in weights)

    def embed(found):
        own = lax.cond(section_index == 0, look_up, lambda: found)
        embedded = own + lax.ppermute(own, "section", [(0, half), (half, 0)])
        return only([half], table_project, (embedded, *own_weights), (4,) + part)

    updated = encode(0, patches.reshape(part), own_weights)
    (found,) = lax.cond(section_index != 0, look_up_and_add, lambda: tuple(nothing(part)))
    swapped = lax.cond(
        section_index >= 2,
        swap_weights,
        lambda *_: tuple(nothing(*[weight.shape for weight in own_weights])),
        after(norm_gain, found),
        *own_weights[1:],
    )
    result = updated
    stream = exchange(after(updated, found, *swapped), "section", pairs)
    (table,) = only([0, half], embed, (after(found, stream),), (4,) + part)
    for even in range(0, section_count, 2):
        odd = even + 1
        returned = None
        if even and even < half:
            updated = encode(odd, stream, swapped)
        elif even == half:
            gain, _, key_weight, value_weight, out_weight = swapped
            shapes = [part] * 4 + ([whole] if odd + 1 < section_count else [])
            first_keys, first_values, keys, values, *memory = only(
                [odd],
                lambda *operands: memory_start(*operands)[: len(shapes)],
                (stream, gain, key_weight, value_weight, norm_gain, w_key[0], w_value[0]),
                *shapes,
            )
            table = exchange(after(table, first_keys), "section", pairs)
            (updated,) = only(
                [odd],
                functools.partial(decoder_end, shipped=True),
                (table[3], out_weight, first_keys, first_values, *table[:3]),
                part,
            )
        elif even > half:
            keys, values = memory_rows(odd, memory[0], swapped)
            updated = decode(odd, stream, keys, values, swapped)
            keys, values = memory_rows(odd, memory[0], own_weights)
        if even:
            returned = exchange(updated, "section", pairs)
            stream = updated
        if even < half:
            updated = encode(odd, stream, own_weights)
        else:
            updated = decode(odd, stream, keys, values, own_weights, (returned,))
        if returned is not None:
            result = jnp.where(section_index == even, returned, result)
        result = jnp.where(section_index == odd, updated, result)
        if odd + 1 < section_count:
            ahead = [(odd, odd + 2), (even, even + 2)]
            if even >= half:
                memory = [exchange(memory[0], "section", ahead)]
            else:
                updated = after(updated, found)
            stream = exchange(updated, "section", ahead)
    return result.reshape(1, micro_count, row_count, width_local)


def solution(mesh):
    return jax.shard_map(
        local,
        mesh=mesh,
        in_specs=(
            P(None, None, "tp"),
            P(),
            P(),
            P("section", "tp"),
            P("section", None),
            P("section", None, "tp"),
            P("section", None, "tp"),
            P("section", None, "tp"),
            P("section", None, "tp"),
        ),
        out_specs=P("section", None, None, "tp"),
        check_vma=False,
    )
```

```python
import functools
import math

import jax
import jax.numpy as jnp
from jax import lax
from jax.experimental import pallas as pl
from jax.experimental.pallas import tpu as pltpu
from jax.sharding import PartitionSpec as P

HEADS = 32


epsilon = 1e-06


CHUNKS = 4


def load_kernel(*refs):
    *refs, sems = refs
    count = len(refs) // 2
    copies = []
    for i, (weight_ref, out_ref) in enumerate(zip(refs[:count], refs[count + 1 :])):
        rows = weight_ref.shape[0] // CHUNKS
        for j in range(CHUNKS):
            part = pl.ds(j * rows, rows)
            copies.append(
                pltpu.make_async_copy(weight_ref.at[part], out_ref.at[part], sems.at[i, j])
            )
    for copy in copies:
        copy.start()
    for copy in copies:
        copy.wait()


def load(weights, moment):
    count = len(weights)
    size = sum(weight.size for weight in weights)
    return pl.pallas_call(
        load_kernel,
        out_shape=[pltpu.VMEM(weight.shape, weight.dtype) for weight in weights],
        in_specs=[pl.BlockSpec(memory_space=pl.ANY)] * (count + 1),
        out_specs=[pl.BlockSpec(memory_space=pltpu.VMEM)] * count,
        scratch_shapes=[pltpu.SemaphoreType.DMA((count, CHUNKS))],
        compiler_params=pltpu.CompilerParams(vmem_limit_bytes=1 << 20),
        cost_estimate=pl.CostEstimate(flops=0, bytes_accessed=4 * size, transcendentals=0),
    )(*weights, moment)


def gather_steps(count):
    bits = [1 << i for i in reversed(range(count.bit_length() - 1))]
    steps = []
    while bits:
        if len(bits) % 2:
            steps.append([bits[0]])
            bits = bits[1:]
        else:
            steps.append([bits[0] | bits[1], bits[1], bits[0]])
            bits = bits[2:]
    return steps


def gather_rows(block, axis, weights=()):
    count = lax.axis_size(axis)
    me = lax.axis_index(axis)
    held = [(block[None], [0])]
    for masks in gather_steps(count):
        if len(held) > 2:
            piece = jnp.concatenate([one for one, _ in held], axis=0)
            held = [(piece, [s for _, sources in held for s in sources])]
        received = []
        for piece, sources in held:
            for mask in masks:
                route = [(i, i ^ mask) for i in range(count)]
                received.append((lax.ppermute(piece, axis, route), [s ^ mask for s in sources]))
        held = held + received
    loaded = load(weights, held[1][0]) if weights else ()
    pieces = {mask: piece[i] for piece, sources in held for i, mask in enumerate(sources)}
    top = count // 2
    swap = (me & top) != 0
    halves = {
        m: jnp.stack(
            [
                jnp.where(swap, pieces[m ^ top], pieces[m]),
                jnp.where(swap, pieces[m], pieces[m ^ top]),
            ]
        )
        for m in range(top)
    }
    bit = top // 2
    while bit:
        swap = (me & bit) != 0
        halves = {m: jnp.where(swap, halves[m ^ bit], halves[m]) for m in halves}
        bit //= 2
    full = jnp.stack([halves[m] for m in range(top)], axis=1)
    full = full.reshape((count,) + block.shape).transpose(1, 0, 2)
    full = full.reshape(block.shape[0], count * block.shape[1])
    return (full, *loaded) if weights else full


def exchange(block, axis, pairs):
    used = [index for pair in pairs for index in pair]
    rest = [index for index in range(lax.axis_size(axis)) if index not in used]
    pairs = list(pairs) + list(zip(rest[0::2], rest[1::2]))
    route = [way for first, second in pairs for way in ((first, second), (second, first))]
    return lax.ppermute(block, axis, route)


def nothing(*shapes, dtype=jnp.bfloat16):
    specs = [pl.BlockSpec(memory_space=pl.ANY)] * len(shapes)
    return pl.pallas_call(
        lambda *refs: None,
        out_shape=[jax.ShapeDtypeStruct(shape, dtype) for shape in shapes],
        out_specs=specs,
    )()


def local(patches, table_ids, lengths, embed_table, norm_gain, w_query, w_key, w_value, w_out):
    section_count = lax.axis_size("section")
    section_index = lax.axis_index("section")
    half = section_count // 2
    micro_count, row_count, width_local = patches.shape
    width_full = w_query.shape[1]
    head_dim = width_full // HEADS
    heads_local = width_local // head_dim
    score_scale = 1.0 / math.sqrt(head_dim)
    own_weights = (norm_gain, w_query[0], w_key[0], w_value[0], w_out[0])
    total_rows = micro_count * row_count
    vocab_local = embed_table.shape[0]
    bf16 = jnp.bfloat16
    part = (total_rows, width_local)
    whole = (total_rows, width_full)

    def member(*indices):
        taken = section_index == indices[0]
        for index in indices[1:]:
            taken = taken | (section_index == index)
        return taken

    def only(indices, body, operands, *shapes):
        return lax.cond(member(*indices), body, lambda *_: tuple(nothing(*shapes)), *operands)

    def after(value, *earlier):
        return lax.optimization_barrier((value,) + earlier)[0]

    def look_up():
        local_ids = table_ids.reshape(-1) - section_index * vocab_local
        vocab_cols = lax.broadcasted_iota(jnp.int32, (total_rows, vocab_local), 1)
        one_hot = (local_ids[:, None] == vocab_cols).astype(bf16)
        return jnp.dot(one_hot, embed_table, preferred_element_type=jnp.float32).astype(bf16)

    def look_up_and_add():
        found = look_up()
        others = list(range(1, section_count))
        total = found
        for shift in range(1, len(others)):
            route = [(s, others[(i + shift) % len(others)]) for i, s in enumerate(others)]
            total = total + lax.ppermute(found, "section", route)
        return (total,)

    def normalise(full, gain):
        values_f = full.astype(jnp.float32)
        inverse = lax.rsqrt(jnp.mean(values_f * values_f, axis=-1, keepdims=True) + epsilon)
        return (values_f * inverse * gain.astype(jnp.float32)).astype(bf16)

    def multiply(rows, weight):
        return jnp.dot(rows, weight, preferred_element_type=jnp.float32)

    def project(full, weights):
        gain, query_weight, key_weight, value_weight = weights
        normed = normalise(full, gain)
        return (
            (multiply(normed, query_weight) * score_scale).astype(bf16),
            multiply(normed, key_weight).astype(bf16),
            multiply(normed, value_weight).astype(bf16),
        )

    def heads_of(rows):
        return rows.reshape(micro_count, row_count, heads_local, head_dim)

    def attend(query, keys, values, mask):
        scores = jnp.einsum("mqhd,mkhd->mhqk", query, keys, preferred_element_type=jnp.float32)
        exp_scores = jnp.where(mask[:, None] > 0, jnp.exp(scores), 0.0)
        weights = (exp_scores / jnp.sum(exp_scores, axis=-1, keepdims=True)).astype(bf16)
        mix = jnp.einsum("mhqk,mkhd->mqhd", weights, values, preferred_element_type=jnp.float32)
        return mix.astype(bf16).reshape(part)

    mask_shape = (micro_count, row_count, row_count)
    wide_mask = (micro_count, row_count, 2 * row_count)

    def patch_mask():
        key_pos = lax.broadcasted_iota(jnp.int32, mask_shape, 2)
        return key_pos < lengths[:, 0][:, None, None]

    def encoder_mask():
        return patch_mask().astype(bf16)

    def decoder_mask():
        query_pos = lax.broadcasted_iota(jnp.int32, mask_shape, 1)
        key_pos = lax.broadcasted_iota(jnp.int32, mask_shape, 2)
        own = (key_pos <= query_pos) & (key_pos < lengths[:, 1][:, None, None])
        return jnp.concatenate([patch_mask(), own], axis=2).astype(bf16)

    def decoder_mix(memory_keys, memory_values, query, keys, values, mask):
        return attend(
            heads_of(query),
            jnp.concatenate([heads_of(memory_keys), heads_of(keys)], axis=1),
            jnp.concatenate([heads_of(memory_values), heads_of(values)], axis=1),
            mask,
        )

    def finish(stream, mix, out_weight, shipped=False):
        if shipped:
            full, out_weight = gather_rows(mix, "tp", (out_weight,))
        else:
            full = gather_rows(mix, "tp")
        change = multiply(full, out_weight)
        return (stream.astype(jnp.float32) + change).astype(bf16)

    def gather_and_project(stream, gain, query_weight, key_weight, value_weight):
        full, *loaded = gather_rows(stream, "tp", (key_weight, value_weight))
        return project(full, (gain, query_weight, *loaded))

    def encoder_start(*operands):
        return (*gather_and_project(*operands), encoder_mask())

    def decoder_start(*operands):
        return (*gather_and_project(*operands), decoder_mask())

    def encoder_end(stream, query, keys, values, mask, out_weight):
        mix = attend(heads_of(query), heads_of(keys), heads_of(values), mask)
        return (finish(stream, mix, out_weight),)

    def decoder_end(stream, out_weight, *heads, shipped=False):
        return (finish(stream, decoder_mix(*heads), out_weight, shipped),)

    def memory_project(memory, gain, key_weight, value_weight):
        normed = normalise(memory, gain)
        keys, values = multiply(normed, key_weight), multiply(normed, value_weight)
        return keys.astype(bf16), values.astype(bf16)

    def memory_start(stream, gain, key_weight, value_weight, *following):
        memory, *shipped = gather_rows(stream, "tp", (key_weight, value_weight))
        first = memory_project(memory, gain, *shipped)
        memory = after(memory, *first)
        return (*first, *memory_project(memory, *following), decoder_mask(), memory)

    def encode(index, stream, weights):
        heads = only([index], encoder_start, (stream, *weights[:4]), part, part, part, mask_shape)
        return only([index], encoder_end, (stream, *heads, weights[4]), part)[0]

    def decode(index, stream, keys, values, weights, earlier=()):
        heads = only([index], decoder_start, (stream, *weights[:4]), part, part, part, wide_mask)
        heads = lax.optimization_barrier((*heads, earlier))[:4]
        return only([index], decoder_end, (stream, weights[4], keys, values, *heads), part)[0]

    def memory_rows(index, memory, weights):
        gain, _, key_weight, value_weight, _ = weights
        operands = (memory, gain, key_weight, value_weight)
        return only([index], memory_project, operands, part, part)

    def table_project(stream, *weights):
        return (jnp.stack(gather_and_project(stream, *weights[:4]) + (stream,)),)

    pairs = [(index, index + 1) for index in range(0, section_count, 2)]

    def swap_weights(*weights):
        route = [way for first, second in pairs[1:] for way in ((first, second), (second, first))]
        return tuple(lax.ppermute(weight, "section", route) for weight in weights)

    def embed(found):
        own = lax.cond(section_index == 0, look_up, lambda: found)
        embedded = own + lax.ppermute(own, "section", [(0, half), (half, 0)])
        return only([half], table_project, (embedded, *own_weights), (4,) + part)

    updated = encode(0, patches.reshape(part), own_weights)
    (found,) = lax.cond(section_index != 0, look_up_and_add, lambda: tuple(nothing(part)))
    swapped = lax.cond(
        section_index >= 2,
        swap_weights,
        lambda *_: tuple(nothing(*[weight.shape for weight in own_weights])),
        after(norm_gain, found),
        *own_weights[1:],
    )
    gain = lax.cond(
        section_index >= 2,
        lambda row: row.astype(jnp.float32),
        lambda row: nothing(row.shape, dtype=jnp.float32)[0],
        swapped[0],
    )
    swapped = (gain, *swapped[1:])
    result = updated
    stream = exchange(after(updated, found, *swapped), "section", pairs)
    (table,) = only([0, half], embed, (after(found, stream),), (4,) + part)
    for even in range(0, section_count, 2):
        odd = even + 1
        returned = None
        if even and even < half:
            updated = encode(odd, stream, swapped)
        elif even == half:
            gain, _, key_weight, value_weight, out_weight = swapped
            shapes = [part] * 4 + [wide_mask] + ([whole] if odd + 1 < section_count else [])
            first_keys, first_values, keys, values, mask, *memory = only(
                [odd],
                lambda *operands: memory_start(*operands)[: len(shapes)],
                (stream, gain, key_weight, value_weight, norm_gain, w_key[0], w_value[0]),
                *shapes,
            )
            table = exchange(after(table, first_keys), "section", pairs)
            (updated,) = only(
                [odd],
                functools.partial(decoder_end, shipped=True),
                (table[3], out_weight, first_keys, first_values, *table[:3], mask),
                part,
            )
        elif even > half:
            keys, values = memory_rows(odd, memory[0], swapped)
            updated = decode(odd, stream, keys, values, swapped)
            keys, values = memory_rows(odd, memory[0], own_weights)
        if even:
            returned = exchange(updated, "section", pairs)
            stream = updated
        if even < half:
            updated = encode(odd, stream, own_weights)
        else:
            updated = decode(odd, stream, keys, values, own_weights, (returned,))
        if returned is not None:
            result = jnp.where(section_index == even, returned, result)
        result = jnp.where(section_index == odd, updated, result)
        if odd + 1 < section_count:
            ahead = [(odd, odd + 2), (even, even + 2)]
            if even >= half:
                memory = [exchange(memory[0], "section", ahead)]
            else:
                updated = after(updated, found)
            stream = exchange(updated, "section", ahead)
    return result.reshape(1, micro_count, row_count, width_local)


def solution(mesh):
    return jax.shard_map(
        local,
        mesh=mesh,
        in_specs=(
            P(None, None, "tp"),
            P(),
            P(),
            P("section", "tp"),
            P("section", None),
            P("section", None, "tp"),
            P("section", None, "tp"),
            P("section", None, "tp"),
            P("section", None, "tp"),
        ),
        out_specs=P("section", None, None, "tp"),
        check_vma=False,
    )
```

```python
import functools
import math

import jax
import jax.numpy as jnp
from jax import lax
from jax.experimental import pallas as pl
from jax.experimental.pallas import tpu as pltpu
from jax.sharding import PartitionSpec as P

HEADS = 32


epsilon = 1e-06


CHUNKS = 4


def load_kernel(*refs):
    *refs, sems = refs
    count = len(refs) // 2
    copies = []
    for i, (weight_ref, out_ref) in enumerate(zip(refs[:count], refs[count + 1 :])):
        rows = weight_ref.shape[0] // CHUNKS
        for j in range(CHUNKS):
            part = pl.ds(j * rows, rows)
            copies.append(
                pltpu.make_async_copy(weight_ref.at[part], out_ref.at[part], sems.at[i, j])
            )
    for copy in copies:
        copy.start()
    for copy in copies:
        copy.wait()


def load(weights, moment):
    count = len(weights)
    size = sum(weight.size for weight in weights)
    return pl.pallas_call(
        load_kernel,
        out_shape=[pltpu.VMEM(weight.shape, weight.dtype) for weight in weights],
        in_specs=[pl.BlockSpec(memory_space=pl.ANY)] * (count + 1),
        out_specs=[pl.BlockSpec(memory_space=pltpu.VMEM)] * count,
        scratch_shapes=[pltpu.SemaphoreType.DMA((count, CHUNKS))],
        compiler_params=pltpu.CompilerParams(vmem_limit_bytes=1 << 20),
        cost_estimate=pl.CostEstimate(flops=0, bytes_accessed=4 * size, transcendentals=0),
    )(*weights, moment)


def gather_steps(count):
    bits = [1 << i for i in reversed(range(count.bit_length() - 1))]
    steps = []
    while bits:
        if len(bits) % 2:
            steps.append([bits[0]])
            bits = bits[1:]
        else:
            steps.append([bits[0] | bits[1], bits[0], bits[1]])
            bits = bits[2:]
    return steps


def gather_rows(block, axis, weights=()):
    count = lax.axis_size(axis)
    me = lax.axis_index(axis)
    held = [(block[None], [0])]
    for masks in gather_steps(count):
        if len(held) > 2:
            piece = jnp.concatenate([one for one, _ in held], axis=0)
            held = [(piece, [s for _, sources in held for s in sources])]
        received = []
        for piece, sources in held:
            for mask in masks:
                route = [(i, i ^ mask) for i in range(count)]
                received.append((lax.ppermute(piece, axis, route), [s ^ mask for s in sources]))
        held = held + received
    loaded = load(weights, held[1][0]) if weights else ()
    pieces = {mask: piece[i] for piece, sources in held for i, mask in enumerate(sources)}
    top = count // 2
    swap = (me & top) != 0
    halves = {
        m: jnp.stack(
            [
                jnp.where(swap, pieces[m ^ top], pieces[m]),
                jnp.where(swap, pieces[m], pieces[m ^ top]),
            ]
        )
        for m in range(top)
    }
    bit = top // 2
    while bit:
        swap = (me & bit) != 0
        halves = {m: jnp.where(swap, halves[m ^ bit], halves[m]) for m in halves}
        bit //= 2
    full = jnp.stack([halves[m] for m in range(top)], axis=1)
    full = full.reshape((count,) + block.shape).transpose(1, 0, 2)
    full = full.reshape(block.shape[0], count * block.shape[1])
    return (full, *loaded) if weights else full


def exchange(block, axis, pairs):
    used = [index for pair in pairs for index in pair]
    rest = [index for index in range(lax.axis_size(axis)) if index not in used]
    pairs = list(pairs) + list(zip(rest[0::2], rest[1::2]))
    route = [way for first, second in pairs for way in ((first, second), (second, first))]
    return lax.ppermute(block, axis, route)


def nothing(*shapes, dtype=jnp.bfloat16):
    specs = [pl.BlockSpec(memory_space=pl.ANY)] * len(shapes)
    return pl.pallas_call(
        lambda *refs: None,
        out_shape=[jax.ShapeDtypeStruct(shape, dtype) for shape in shapes],
        out_specs=specs,
    )()


def local(patches, table_ids, lengths, embed_table, norm_gain, w_query, w_key, w_value, w_out):
    section_count = lax.axis_size("section")
    section_index = lax.axis_index("section")
    half = section_count // 2
    micro_count, row_count, width_local = patches.shape
    width_full = w_query.shape[1]
    head_dim = width_full // HEADS
    heads_local = width_local // head_dim
    score_scale = 1.0 / math.sqrt(head_dim)
    own_weights = (norm_gain, w_query[0], w_key[0], w_value[0], w_out[0])
    total_rows = micro_count * row_count
    vocab_local = embed_table.shape[0]
    bf16 = jnp.bfloat16
    part = (total_rows, width_local)
    whole = (total_rows, width_full)

    def member(*indices):
        taken = section_index == indices[0]
        for index in indices[1:]:
            taken = taken | (section_index == index)
        return taken

    def only(indices, body, operands, *shapes):
        return lax.cond(member(*indices), body, lambda *_: tuple(nothing(*shapes)), *operands)

    def after(value, *earlier):
        return lax.optimization_barrier((value,) + earlier)[0]

    def look_up():
        local_ids = table_ids.reshape(-1) - section_index * vocab_local
        vocab_cols = lax.broadcasted_iota(jnp.int32, (total_rows, vocab_local), 1)
        one_hot = (local_ids[:, None] == vocab_cols).astype(bf16)
        return jnp.dot(one_hot, embed_table, preferred_element_type=jnp.float32).astype(bf16)

    def look_up_and_add():
        found = look_up()
        others = list(range(1, section_count))
        total = found
        for shift in range(1, len(others)):
            route = [(s, others[(i + shift) % len(others)]) for i, s in enumerate(others)]
            total = total + lax.ppermute(found, "section", route)
        return (total,)

    def normalise(full, gain):
        values_f = full.astype(jnp.float32)
        inverse = lax.rsqrt(jnp.mean(values_f * values_f, axis=-1, keepdims=True) + epsilon)
        return (values_f * inverse * gain.astype(jnp.float32)).astype(bf16)

    def multiply(rows, weight):
        return jnp.dot(rows, weight, preferred_element_type=jnp.float32)

    def project(full, weights):
        gain, query_weight, key_weight, value_weight = weights
        normed = normalise(full, gain)
        return (
            (multiply(normed, query_weight) * score_scale).astype(bf16),
            multiply(normed, key_weight).astype(bf16),
            multiply(normed, value_weight).astype(bf16),
        )

    def heads_of(rows):
        return rows.reshape(micro_count, row_count, heads_local, head_dim)

    def attend(query, keys, values, mask):
        scores = jnp.einsum("mqhd,mkhd->mhqk", query, keys, preferred_element_type=jnp.float32)
        exp_scores = jnp.where(mask[:, None], jnp.exp(scores), 0.0)
        weights = (exp_scores / jnp.sum(exp_scores, axis=-1, keepdims=True)).astype(bf16)
        mix = jnp.einsum("mhqk,mkhd->mqhd", weights, values, preferred_element_type=jnp.float32)
        return mix.astype(bf16).reshape(part)

    mask_shape = (micro_count, row_count, row_count)

    def patch_mask():
        key_pos = lax.broadcasted_iota(jnp.int32, mask_shape, 2)
        return key_pos < lengths[:, 0][:, None, None]

    def encoder_mix(query, keys, values):
        return attend(heads_of(query), heads_of(keys), heads_of(values), patch_mask())

    def decoder_mix(memory_keys, memory_values, query, keys, values):
        query_pos = lax.broadcasted_iota(jnp.int32, mask_shape, 1)
        key_pos = lax.broadcasted_iota(jnp.int32, mask_shape, 2)
        own = (key_pos <= query_pos) & (key_pos < lengths[:, 1][:, None, None])
        return attend(
            heads_of(query),
            jnp.concatenate([heads_of(memory_keys), heads_of(keys)], axis=1),
            jnp.concatenate([heads_of(memory_values), heads_of(values)], axis=1),
            jnp.concatenate([patch_mask(), own], axis=2),
        )

    def finish(stream, mix, out_weight, shipped=False):
        if shipped:
            full, out_weight = gather_rows(mix, "tp", (out_weight,))
        else:
            full = gather_rows(mix, "tp")
        change = multiply(full, out_weight)
        return (stream.astype(jnp.float32) + change).astype(bf16)

    def gather_and_project(stream, gain, query_weight, key_weight, value_weight):
        full, *loaded = gather_rows(stream, "tp", (key_weight, value_weight))
        return project(full, (gain, query_weight, *loaded))

    def encoder_end(stream, query, keys, values, out_weight):
        return (finish(stream, encoder_mix(query, keys, values), out_weight),)

    def decoder_end(stream, out_weight, *heads, shipped=False):
        return (finish(stream, decoder_mix(*heads), out_weight, shipped),)

    def memory_project(memory, gain, key_weight, value_weight):
        normed = normalise(memory, gain)
        keys, values = multiply(normed, key_weight), multiply(normed, value_weight)
        return keys.astype(bf16), values.astype(bf16)

    def memory_start(stream, gain, key_weight, value_weight, next_gain):
        memory, *shipped = gather_rows(stream, "tp", (key_weight, value_weight))
        first = memory_project(memory, gain, *shipped)
        return (*first, lax.optimization_barrier(normalise(memory, next_gain)), memory)

    def both_project(stream, ready, gain, query_weight, key_weight, value_weight):
        full, key_weight, value_weight = gather_rows(stream, "tp", (key_weight, value_weight))
        normed = normalise(full, gain)
        rows = jnp.concatenate([ready, normed], axis=0)
        query = (multiply(normed, query_weight) * score_scale).astype(bf16)
        keys = multiply(rows, key_weight).astype(bf16)
        values = multiply(rows, value_weight).astype(bf16)
        return (
            keys[:total_rows],
            values[:total_rows],
            query,
            keys[total_rows:],
            values[total_rows:],
        )

    def encode(index, stream, weights):
        heads = only([index], gather_and_project, (stream, *weights[:4]), part, part, part)
        return only([index], encoder_end, (stream, *heads, weights[4]), part)[0]

    def decode(index, stream, keys, values, weights, earlier=()):
        heads = only([index], gather_and_project, (stream, *weights[:4]), part, part, part)
        heads = lax.optimization_barrier((*heads, earlier))[:3]
        return only([index], decoder_end, (stream, weights[4], keys, values, *heads), part)[0]

    def decode_both(index, stream, ready, weights, earlier):
        heads = only([index], both_project, (stream, ready, *weights[:4]), *[part] * 5)
        heads = lax.optimization_barrier((*heads, earlier))[:5]
        return only([index], decoder_end, (stream, weights[4], *heads), part)[0]

    def memory_rows(index, memory, weights):
        gain, _, key_weight, value_weight, _ = weights
        operands = (memory, gain, key_weight, value_weight)
        return only([index], memory_project, operands, part, part)

    def table_project(stream, *weights):
        return (jnp.stack(gather_and_project(stream, *weights[:4]) + (stream,)),)

    pairs = [(index, index + 1) for index in range(0, section_count, 2)]

    def swap_weights(*weights):
        route = [way for first, second in pairs[1:] for way in ((first, second), (second, first))]
        return tuple(lax.ppermute(weight, "section", route) for weight in weights)

    def embed(found):
        own = lax.cond(section_index == 0, look_up, lambda: found)
        embedded = own + lax.ppermute(own, "section", [(0, half), (half, 0)])
        return only([half], table_project, (embedded, *own_weights), (4,) + part)

    updated = encode(0, patches.reshape(part), own_weights)
    (found,) = lax.cond(section_index != 0, look_up_and_add, lambda: tuple(nothing(part)))
    swapped = lax.cond(
        section_index >= 2,
        swap_weights,
        lambda *_: tuple(nothing(*[weight.shape for weight in own_weights])),
        after(norm_gain, found),
        *own_weights[1:],
    )
    gain = lax.cond(
        section_index >= 2,
        lambda row: row.astype(jnp.float32),
        lambda row: nothing(row.shape, dtype=jnp.float32)[0],
        swapped[0],
    )
    swapped = (gain, *swapped[1:])
    result = updated
    stream = exchange(after(updated, found, *swapped), "section", pairs)
    (table,) = only([0, half], embed, (after(found, stream),), (4,) + part)
    for even in range(0, section_count, 2):
        odd = even + 1
        returned = None
        if even and even < half:
            updated = encode(odd, stream, swapped)
        elif even == half:
            gain, _, key_weight, value_weight, out_weight = swapped
            shapes = [part, part, whole] + ([whole] if odd + 1 < section_count else [])
            first_keys, first_values, ready, *memory = only(
                [odd],
                lambda *operands: memory_start(*operands)[: len(shapes)],
                (stream, gain, key_weight, value_weight, norm_gain),
                *shapes,
            )
            table = exchange(after(table, first_keys), "section", pairs)
            (updated,) = only(
                [odd],
                functools.partial(decoder_end, shipped=True),
                (table[3], out_weight, first_keys, first_values, *table[:3]),
                part,
            )
        elif even > half:
            keys, values = memory_rows(odd, memory[0], swapped)
            updated = decode(odd, stream, keys, values, swapped)
            keys, values = memory_rows(odd, memory[0], own_weights)
        if even:
            returned = exchange(updated, "section", pairs)
            stream = updated
        if even < half:
            updated = encode(odd, stream, own_weights)
        elif even == half:
            updated = decode_both(odd, stream, ready, own_weights, (returned,))
        else:
            updated = decode(odd, stream, keys, values, own_weights, (returned,))
        if returned is not None:
            result = jnp.where(section_index == even, returned, result)
        result = jnp.where(section_index == odd, updated, result)
        if odd + 1 < section_count:
            ahead = [(odd, odd + 2), (even, even + 2)]
            if even >= half:
                memory = [exchange(memory[0], "section", ahead)]
            else:
                updated = after(updated, found)
            stream = exchange(updated, "section", ahead)
    return result.reshape(1, micro_count, row_count, width_local)


def solution(mesh):
    return jax.shard_map(
        local,
        mesh=mesh,
        in_specs=(
            P(None, None, "tp"),
            P(),
            P(),
            P("section", "tp"),
            P("section", None),
            P("section", None, "tp"),
            P("section", None, "tp"),
            P("section", None, "tp"),
            P("section", None, "tp"),
        ),
        out_specs=P("section", None, None, "tp"),
        check_vma=False,
    )
```
